32 devices in a mesh: clips: 2 (over x), tm: 8 (over z, y), cols: 2 (over core).
Axes of the slice: x: 2, y: 2, z: 4, core: 2. Of those that a mesh axis runs over, the one named last changes fastest.
Arguments:
- video: bfloat16 [64, 32, 32, 512], P(('clips', 'tm'), None, 'cols'), parts along dimension 0, may hold values from -6 to 6
- w_time: bfloat16 [3, 512, 512], replicated, may hold values from -0.15625 to 0.15625
- b_time: float32 [512], replicated, may hold values from -3 to 3
- w_down: bfloat16 [3, 512, 512], replicated, may hold values from -0.15625 to 0.15625
- b_down: float32 [512], replicated, may hold values from -3 to 3
- w_space: bfloat16 [9, 512, 512], replicated, may hold values from -0.09375 to 0.09375
- b_space: float32 [512], replicated, may hold values from -3 to 3
- gain: float32 [512], replicated, may hold values from 0.1 to 1.9
- w_query: bfloat16 [512, 512], replicated, may hold values from -30 to 30
- w_key: bfloat16 [512, 512], replicated, may hold values from -0.25 to 0.25
- w_value: bfloat16 [512, 512], replicated, may hold values from -0.25 to 0.25
- w_out: bfloat16 [512, 512], replicated, may hold values from -0.25 to 0.25
Outputs:
- encoded: bfloat16 [32, 32, 32, 512], P(('clips', 'tm'), None, 'cols'), parts along dimension 0
The draws below stay inside these ranges and needn't reach their ends.
There are 2 independent parts, one for each index of `clips`. The reference program is written for one: setup_inputs(seed, part) draws one part's arguments, and reference() takes and returns one part's arrays. A program takes and returns all parts, laid end to end along the dimension named above; an argument that names none is the same for every part. Nothing has to cross between parts.
All inputs are finite; a program needn't handle non-finite values.
Results may differ from the reference program's by a relative error of at most 0.019.
The reference program's roundings to bfloat16 on the way (of `lifted`, `reduced`, `spatial`, `normed`, `query`, `probs` and `context`) count: a program that leaves them out, or rounds other values in their place, can miss the bound.
Values may be sent and summed in bfloat16 or wider, within the bound.
A program may use at most 64 MiB of HBM per device.

```python
import jax
import jax.numpy as jnp
from jax import lax

C = 512
H = 32
W = 32
FRAMES = 32


def draw_w_query(key, part):
    values = jax.random.truncated_normal(key, -4.0, 4.0, (C, C), jnp.float32) * C ** (-0.5)
    return values.astype(jnp.bfloat16)


def block_levels(stream_key, extent, shards, smallest, high):
    def one(position, parts):
        steps = jax.random.uniform(jax.random.fold_in(jax.random.fold_in(stream_key, 6), position), (parts,), jnp.float32, smallest / len(shards), high / len(shards))
        return jnp.repeat(jnp.exp(steps), extent[position] // parts).reshape((-1,) + (1,) * (len(extent) - position - 1))

    factor_of = one(*shards[0])
    for cut in shards[1:]:
        factor_of = factor_of * one(*cut)
    return factor_of


def gaussian(key, dims, scale, most, pieces=(), kind=jnp.bfloat16):
    entries = scale * jax.random.normal(key, dims, jnp.float32)
    if pieces:
        entries = entries * block_levels(key, dims, pieces, -0.22, 0.18)
    return jnp.clip(entries, -most, most).astype(kind)


def setup_inputs(seed: int = 0, part: int = 0) -> dict:
    streams_of = jax.random.split(jax.random.key(seed), 13)
    part_keys = jax.random.split(jax.random.fold_in(streams_of[12], part), 13)
    video = gaussian(part_keys[0], (FRAMES, H, W, C), 1.0, 6.0, ((0, 8), (2, 2)))
    w_time = gaussian(streams_of[1], (3, C, C), (3 * C) ** -0.5, 0.15625)
    b_time = gaussian(streams_of[2], (C,), 0.5, 3.0, (), jnp.float32)
    w_down = gaussian(streams_of[3], (3, C, C), (3 * C) ** -0.5, 0.15625)
    b_down = gaussian(streams_of[4], (C,), 0.5, 3.0, (), jnp.float32)
    w_space = gaussian(streams_of[5], (9, C, C), (9 * C) ** -0.5, 0.09375)
    b_space = gaussian(streams_of[6], (C,), 0.5, 3.0, (), jnp.float32)
    gain = jnp.clip(1.0 + 0.18 * jax.random.normal(streams_of[7], (C,), jnp.float32), 0.1, 1.9)
    w_query = draw_w_query(jax.random.fold_in(streams_of[12], 71), part)
    w_key = gaussian(streams_of[9], (C, C), C ** -0.5, 0.25)
    w_value = gaussian(streams_of[10], (C, C), C ** -0.5, 0.25)
    w_out = gaussian(streams_of[11], (C, C), C ** -0.5, 0.25)
    return {"video": video, "w_time": w_time, "b_time": b_time, "w_down": w_down, "b_down": b_down, "w_space": w_space, "b_space": b_space, "gain": gain, "w_query": w_query, "w_key": w_key, "w_value": w_value, "w_out": w_out}


epsilon = 1e-06

def attend(sequence, gain, w_query, w_key, w_value, w_out):
    frames, pixels, channels = sequence.shape
    wide = sequence.astype(jnp.float32)
    scale = lax.rsqrt(lax.optimization_barrier(jnp.mean(wide * wide, axis=-1, keepdims=True)) + epsilon)
    normed = (wide * scale * gain).astype(jnp.bfloat16).reshape(-1, channels)
    query = jnp.dot(normed, w_query, preferred_element_type=jnp.float32).astype(jnp.bfloat16).reshape(frames, pixels, channels)
    key = jnp.dot(normed, w_key, preferred_element_type=jnp.float32).astype(jnp.bfloat16).reshape(frames, pixels, channels)
    value = jnp.dot(normed, w_value, preferred_element_type=jnp.float32).astype(jnp.bfloat16).reshape(frames, pixels, channels)
    scores = jnp.einsum('spc,tpc->pst', query.astype(jnp.float32), key.astype(jnp.float32)) * channels ** (-0.5)
    steps = jnp.arange(frames)
    allowed = steps[None, :] <= steps[:, None]
    scores = jnp.where(allowed[None], scores, -1e+30)
    largest = lax.optimization_barrier(jnp.max(scores, axis=-1, keepdims=True))
    probs = jnp.exp(scores - largest)
    probs = probs / lax.optimization_barrier(jnp.sum(probs, axis=-1, keepdims=True))
    probs = probs.astype(jnp.bfloat16)
    context = jnp.einsum('pst,tpc->spc', probs.astype(jnp.float32), value.astype(jnp.float32)).astype(jnp.bfloat16)
    mixed = jnp.dot(context.reshape(-1, channels), w_out, preferred_element_type=jnp.float32).reshape(frames, pixels, channels)
    return (wide + mixed).astype(jnp.bfloat16)

def reference(video, w_time, b_time, w_down, b_down, w_space, b_space, gain, w_query, w_key, w_value, w_out):
    frames, height, columns, channels = video.shape
    shape = (frames, height, columns, channels)
    padded = jnp.concatenate([jnp.zeros((2, height, columns, channels), video.dtype), video], 0)
    summed = jnp.zeros((frames * height * columns, channels), jnp.float32) + b_time
    for offset in range(3):
        summed = summed + jnp.dot(padded[2 - offset:2 - offset + frames].reshape(-1, channels), w_time[offset], preferred_element_type=jnp.float32)
    lifted = (video.astype(jnp.float32) + jax.nn.silu(summed.reshape(shape))).astype(jnp.bfloat16)
    shifted = jnp.concatenate([jnp.zeros((1, height, columns, channels), lifted.dtype), lifted], 0)
    halves = frames // 2
    taps = [shifted[2:frames + 1:2], shifted[1:frames:2], shifted[0:frames - 1:2]]
    summed = jnp.zeros((halves * height * columns, channels), jnp.float32) + b_down
    for offset in range(3):
        summed = summed + jnp.dot(taps[offset].reshape(-1, channels), w_down[offset], preferred_element_type=jnp.float32)
    reduced = summed.reshape(halves, height, columns, channels).astype(jnp.bfloat16)
    framed = jnp.pad(reduced, ((0, 0), (1, 1), (1, 1), (0, 0)))
    summed = jnp.zeros((halves * height * columns, channels), jnp.float32) + b_space
    for row_tap in range(3):
        for col_tap in range(3):
            window = framed[:, row_tap:row_tap + height, col_tap:col_tap + columns]
            summed = summed + jnp.dot(window.reshape(-1, channels), w_space[3 * row_tap + col_tap], preferred_element_type=jnp.float32)
    spatial = (reduced.astype(jnp.float32) + jax.nn.silu(summed.reshape(halves, height, columns, channels))).astype(jnp.bfloat16)
    encoded = attend(spatial.reshape(halves, height * columns, channels), gain, w_query, w_key, w_value, w_out)
    return encoded.reshape(halves, height, columns, channels)
```

```python
from functools import partial

import jax
import jax.numpy as jnp
from jax import lax
from jax.experimental import pallas as pl
from jax.experimental.pallas import tpu as pltpu
from jax.sharding import PartitionSpec as P

epsilon = 1e-06
MESH = pl.DeviceIdType.MESH


def block_kernel(
    shape, video_hbm, wt_hbm, bt, wd_hbm, bd, ws_hbm, bs, gain, wq_hbm, wk_hbm, wv_hbm, wo_hbm, y_ref,
    wt, wd, ws, wq, wk, wv, wo, video, lifted, left_of, middle, right_of,
    edges, halo, relayed, spatial, held, done,
    load_sem, up_send, up_recv, down_send, down_recv, pass_send, pass_recv, edge_send, edge_recv,
    send_sem, recv_sem, back_sem, home_sem,
):
    height, strip = shape
    frames, area, channels = video_hbm.shape
    halves, chunks, owners, pixels, _ = y_ref.shape
    total = owners * halves
    rows = total * pixels
    me, col, cols = lax.axis_index("tm"), lax.axis_index("cols"), lax.axis_size("cols")
    f32, bf16 = jnp.float32, jnp.bfloat16
    bands, padded = edges.shape[1], edges.shape[3]
    share = chunks // bands
    lines = height // bands
    starts = [0] + [b * lines + 1 for b in range(1, bands)] + [height]
    relays = owners % 2 == 0 and owners > 2

    loads = [
        pltpu.make_async_copy(source, target, load_sem.at[i])
        for i, (source, target) in enumerate(
            (
                (video_hbm, video.at[pl.ds(1, frames)]), (wt_hbm, wt), (wd_hbm, wd), (ws_hbm, ws),
                (wq_hbm, wq), (wk_hbm, wk), (wv_hbm, wv), (wo_hbm, wo),
            )
        )
    ]
    for load in loads:
        load.start()

    barrier = pltpu.get_barrier_semaphore()

    def greet(k, _):
        peer = lax.rem(me + k, owners)
        pl.semaphore_signal(barrier, inc=1, device_id={"tm": peer}, device_id_type=MESH)
        return 0

    lax.fori_loop(1, owners, greet, 0)

    def greet_side(k, _):
        peer = lax.rem(col + k, cols)
        pl.semaphore_signal(barrier, inc=1, device_id={"cols": peer}, device_id_type=MESH)
        return 0

    lax.fori_loop(1, cols, greet_side, 0)

    for j in range(halves + 1):
        for shifted in (left_of, middle, right_of):
            for line in (0, height + 1):
                shifted[j, line] = jnp.zeros((strip, channels), bf16)

    has_next, has_before = me < owners - 1, me > 0
    even = lax.rem(me, 2) == 0

    @pl.when(jnp.logical_not(has_before))
    def _():
        video[0] = jnp.zeros((area, channels), bf16)

    @pl.when(jnp.logical_not(has_next))
    def _():
        for i in range(2):
            video[frames + 1 + i] = jnp.zeros((area, channels), bf16)

    pl.semaphore_wait(barrier, owners + cols - 2)

    def span(b):
        return pl.ds(starts[b] * strip, (starts[b + 1] - starts[b]) * strip)

    def remote(source, target, sent, landed, peer):
        return pltpu.make_async_remote_copy(
            src_ref=source, dst_ref=target, send_sem=sent, recv_sem=landed,
            device_id={"tm": peer}, device_id_type=MESH,
        )

    def upward(b):
        peer = lax.rem(me + 1, owners)
        return remote(video.at[frames, span(b)], video.at[0, span(b)], up_send.at[b], up_recv.at[b], peer)

    def downward(i, b):
        peer = lax.rem(me + owners - 1, owners)
        return remote(
            video.at[1 + i, span(b)], video.at[frames + 1 + i, span(b)],
            down_send.at[i, b], down_recv.at[i, b], peer,
        )

    def aside(b):
        peer = lax.rem(me + 1, owners)
        return remote(video.at[2, span(b)], relayed.at[span(b)], down_send.at[1, b], pass_recv.at[b], peer)

    def onward(b):
        peer = lax.rem(me + owners - 2, owners)
        return remote(
            relayed.at[span(b)], video.at[frames + 2, span(b)], pass_send.at[b], down_recv.at[1, b], peer
        )

    turns = even & has_before if relays else me < 0
    passes = jnp.logical_not(even) & (me > 2) if relays else me < 0
    straight = has_before & jnp.logical_not(turns)

    def send_halos():
        for b in range(bands):
            @pl.when(has_next)
            def _():
                upward(b).start()
        for b in range(bands):
            @pl.when(has_before)
            def _():
                downward(0, b).start()

            @pl.when(straight)
            def _():
                downward(1, b).start()

            @pl.when(turns)
            def _():
                aside(b).start()

    def pass_on(b):
        @pl.when(passes)
        def _():
            aside(b).wait_recv()
            onward(b).start()

    def stacked(ref, which, b):
        return jnp.concatenate([ref[f, span(b)] for f in which], 0)

    def lift(first, count, b):
        size = (starts[b + 1] - starts[b]) * strip
        own = [f + 1 for f in range(first, first + count)]
        summed = jnp.dot(stacked(video, own, b), wt[0], preferred_element_type=f32)
        for k in (1, 2) if first else ():
            summed = summed + jnp.dot(
                stacked(video, [f - k for f in own], b), wt[k], preferred_element_type=f32
            )
        summed = summed + bt[...]
        result = (stacked(video, own, b).astype(f32) + jax.nn.silu(summed)).astype(bf16)
        for i in range(count):
            lifted[first + i, span(b)] = result[i * size : (i + 1) * size]

    def sideways(j, b, side):
        peer = lax.rem(col + 1, cols) if side == 0 else lax.rem(col + cols - 1, cols)
        return pltpu.make_async_remote_copy(
            src_ref=edges.at[j, b, side], dst_ref=halo.at[j, b, side],
            send_sem=edge_send.at[j, b, side], recv_sem=edge_recv.at[j, b, side],
            device_id={"cols": peer}, device_id_type=MESH,
        )

    sends_side = (col < cols - 1, col > 0)
    takes_side = (col > 0, col < cols - 1)

    def window(ref, j, start, count):
        return ref[j, start : start + count].reshape(count * strip, channels)

    def reduce_band(j, b):
        first, last = starts[b], starts[b + 1]
        count = last - first
        summed = jnp.zeros((count * strip, channels), f32) + bd[...]
        for k in range(3 if j else 2):
            summed = summed + jnp.dot(
                lifted[2 * j + 1 - k, span(b)], wd[k], preferred_element_type=f32
            )
        reduced = summed.astype(bf16)
        middle[j, 1 + first : 1 + last] = reduced.reshape(count, strip, channels)
        wide = reduced.astype(f32).reshape(count, strip, channels)
        rest = jnp.zeros((padded - count, channels), f32)
        for side, place in ((0, strip - 1), (1, 0)):
            column = wide[:, place]
            column = jnp.concatenate([column, rest], 0) if padded > count else column
            edges[j, b, side] = column.astype(bf16)
        for side in range(2):
            @pl.when(sends_side[side])
            def _():
                sideways(j, b, side).start()

    def shift_band(j, b):
        for side in range(2):
            @pl.when(takes_side[side])
            def _():
                sideways(j, b, side).wait_recv()

            @pl.when(jnp.logical_not(takes_side[side]))
            def _():
                halo[j, b, side] = jnp.zeros((padded, channels), bf16)

        first, last = starts[b], starts[b + 1]
        count = last - first
        size = count * strip
        wide = window(middle, j, 1 + first, count).astype(f32)
        place = lax.rem(lax.broadcasted_iota(jnp.int32, (size, channels), 0), strip)

        def spread(side):
            column = halo[j, b, side].astype(f32)[:count]
            column = jnp.broadcast_to(column[:, None, :], (count, strip, channels))
            return column.reshape(size, channels)

        lower = jnp.where(place == 0, spread(0), pltpu.roll(wide, 1, 0))
        upper = jnp.where(place == strip - 1, spread(1), pltpu.roll(wide, size - 1, 0))
        left_of[j, 1 + first : 1 + last] = lower.astype(bf16).reshape(count, strip, channels)
        right_of[j, 1 + first : 1 + last] = upper.astype(bf16).reshape(count, strip, channels)

    def convolve_band(j, b):
        first = b * lines
        summed = jnp.zeros((lines * strip, channels), f32) + bs[...]
        for k, shifted in ((1, middle), (0, left_of), (2, right_of)):
            for a in range(3):
                summed = summed + jnp.dot(
                    window(shifted, j, first + a, lines), ws[3 * a + k], preferred_element_type=f32
                )
        result = (window(middle, j, 1 + first, lines).astype(f32) + jax.nn.silu(summed)).astype(bf16)
        spatial[j, b * share : (b + 1) * share] = result.reshape(share, owners, pixels, channels)

    def outward(j, c, peer, slot, frame):
        return remote(
            spatial.at[j, c, peer], held.at[c, frame], send_sem.at[j, c, slot], recv_sem.at[c, frame], peer
        )

    def homeward(c, peer, slot, source):
        return remote(
            done.at[c, peer], y_ref.at[:, c, source], back_sem.at[c, slot], home_sem.at[c, source], peer
        )

    def in_use(j):
        return me == 0 if j == 0 else has_next if j == halves else me >= 0

    def scatter(j, c):
        def send(k, _):
            outward(j, c, lax.rem(me + k, owners), k, halves * me + j).start()
            return 0

        @pl.when(in_use(j))
        def _():
            lax.fori_loop(1, owners, send, 0)

    def attend(c):
        for j in range(halves + 1):
            @pl.when(in_use(j))
            def _():
                held[c, halves * me + j] = spatial[j, c, me]

        def arrive(f, _):
            source = lax.div(jnp.maximum(f - 1, 0), halves)

            @pl.when(source != me)
            def _():
                outward(0, c, lax.rem(me + 1, owners), 0, f).wait_recv()

            return 0

        lax.fori_loop(0, total, arrive, 0)
        place = lax.broadcasted_iota(jnp.int32, (rows, rows), 0)
        other = lax.broadcasted_iota(jnp.int32, (rows, rows), 1)
        allowed = (lax.rem(place, pixels) == lax.rem(other, pixels)) & (other <= place)
        wide = held[c].reshape(rows, channels).astype(f32)
        scale = lax.rsqrt(jnp.mean(wide * wide, axis=-1, keepdims=True) + epsilon)
        normed = (wide * scale * gain[...]).astype(bf16)
        query = jnp.dot(normed, wq[...], preferred_element_type=f32).astype(bf16)
        key = jnp.dot(normed, wk[...], preferred_element_type=f32).astype(bf16)
        value = jnp.dot(normed, wv[...], preferred_element_type=f32).astype(bf16)
        scores = lax.dot_general(
            query, key, (((1,), (1,)), ((), ())), preferred_element_type=f32
        ) * channels ** (-0.5)
        scores = jnp.where(allowed, scores, -1e30)
        largest = jnp.max(scores, axis=-1, keepdims=True)
        probs = jnp.exp(scores - largest)
        probs = (probs / jnp.sum(probs, axis=-1, keepdims=True)).astype(bf16)
        context = jnp.dot(probs, value, preferred_element_type=f32).astype(bf16)
        mixed = jnp.dot(context, wo[...], preferred_element_type=f32)
        result = (wide + mixed).astype(bf16)
        done[c] = result.reshape(owners, halves, pixels, channels)

        def back(k, _):
            homeward(c, lax.rem(me + k, owners), k, me).start()
            return 0

        lax.fori_loop(1, owners, back, 0)
        y_ref[:, c, me] = done[c, me]

    loads[0].wait()
    send_halos()
    for load in loads[1:]:
        load.wait()

    def finish_band(j, b):
        shift_band(j, b)
        convolve_band(j, b)
        for c in range(b * share, (b + 1) * share):
            scatter(j, c)

    @pl.when(jnp.logical_not(has_before))
    def _():
        for b in range(bands):
            lift(0, 1, b)
            lift(1, 1, b)
            reduce_band(0, b)
        for b in range(bands):
            finish_band(0, b)

    lift(2, frames - 2, 0)
    for j in range(1, halves + 1):
        for b in range(bands):
            if j == halves:
                pass_on(b)
            if j == 1:
                @pl.when(has_before)
                def _():
                    upward(b).wait_recv()
                    lift(1, 1, b)
            if j == halves:
                @pl.when(has_next)
                def _():
                    for i in range(2):
                        downward(i, b).wait_recv()

                lift(frames, 2, b)
            reduce_band(j, b)
            if j == 1 and b + 1 < bands:
                lift(2, frames - 2, b + 1)
            finish_band(j, b)
    for c in range(chunks):
        attend(c)

    for b in range(bands):
        @pl.when(has_next)
        def _():
            upward(b).wait_send()

        @pl.when(has_before)
        def _():
            for i in range(2):
                downward(i, b).wait_send()

        @pl.when(passes)
        def _():
            onward(b).wait_send()

    for j in range(halves + 1):
        for b in range(bands):
            for side in range(2):
                @pl.when(sends_side[side] & (me == 0) if j == 0 else sends_side[side])
                def _():
                    sideways(j, b, side).wait_send()

    for c in range(chunks):
        for j in range(halves + 1):
            def left(k, _):
                outward(j, c, lax.rem(me + k, owners), k, 0).wait_send()
                return 0

            @pl.when(in_use(j))
            def _():
                lax.fori_loop(1, owners, left, 0)

        def finish(k, _):
            peer, source = lax.rem(me + k, owners), lax.rem(me + owners - k, owners)
            homeward(c, peer, k, me).wait_send()
            homeward(c, peer, k, source).wait_recv()
            return 0

        lax.fori_loop(1, owners, finish, 0)


def per_device(
    video, w_time, b_time, w_down, b_down, w_space, b_space, gain, w_query, w_key, w_value, w_out
):
    frames, height, strip, channels = video.shape
    halves, owners, area = frames // 2, lax.axis_size("tm"), height * strip
    owned = area // owners
    pixels = min(16, owned)
    chunks = owned // pixels
    bands = 2 if chunks % 2 == 0 else 1
    padded = -(-(height // bands + bands - 1) // 8) * 8
    vmem = pl.BlockSpec(memory_space=pltpu.VMEM)
    hbm = pl.BlockSpec(memory_space=pltpu.HBM)
    bf16 = jnp.bfloat16
    square = (channels, channels)
    slots = halves + 1
    shifted = pltpu.VMEM((slots, height + 2, strip, channels), bf16)
    flat = lambda v: v.reshape(1, channels)
    sems = pltpu.SemaphoreType.DMA
    result = pl.pallas_call(
        partial(block_kernel, (height, strip)),
        out_shape=jax.ShapeDtypeStruct((halves, chunks, owners, pixels, channels), bf16),
        in_specs=[hbm, hbm, vmem, hbm, vmem, hbm, vmem, vmem, hbm, hbm, hbm, hbm],
        out_specs=vmem,
        scratch_shapes=[
            pltpu.VMEM((3,) + square, bf16),
            pltpu.VMEM((3,) + square, bf16),
            pltpu.VMEM((9,) + square, bf16),
            pltpu.VMEM(square, bf16),
            pltpu.VMEM(square, bf16),
            pltpu.VMEM(square, bf16),
            pltpu.VMEM(square, bf16),
            pltpu.VMEM((frames + 3, area, channels), bf16),
            pltpu.VMEM((frames + 2, area, channels), bf16),
            shifted,
            shifted,
            shifted,
            pltpu.VMEM((slots, bands, 2, padded, channels), bf16),
            pltpu.VMEM((slots, bands, 2, padded, channels), bf16),
            pltpu.VMEM((area, channels), bf16),
            pltpu.VMEM((slots, chunks, owners, pixels, channels), bf16),
            pltpu.VMEM((chunks, owners * halves, pixels, channels), bf16),
            pltpu.VMEM((chunks, owners, halves, pixels, channels), bf16),
            sems((8,)),
            sems((bands,)),
            sems((bands,)),
            sems((2, bands)),
            sems((2, bands)),
            sems((bands,)),
            sems((bands,)),
            sems((slots, bands, 2)),
            sems((slots, bands, 2)),
            sems((slots, chunks, owners)),
            sems((chunks, owners * halves)),
            sems((chunks, owners)),
            sems((chunks, owners)),
        ],
        compiler_params=pltpu.CompilerParams(
            collective_id=0, has_side_effects=True, vmem_limit_bytes=57 * 1024 * 1024
        ),
    )(
        video.reshape(frames, area, channels), w_time, flat(b_time), w_down, flat(b_down),
        w_space, flat(b_space), flat(gain), w_query, w_key, w_value, w_out,
    )
    return result.reshape(halves, height, strip, channels)


def solution(mesh):
    return jax.shard_map(
        per_device,
        mesh=mesh,
        in_specs=(P(("clips", "tm"), None, "cols", None),) + (P(),) * 11,
        out_specs=P(("clips", "tm"), None, "cols", None),
        check_vma=False,
    )
```

```python
import jax
import jax.numpy as jnp
from jax import lax
from jax.experimental import pallas as pl
from jax.experimental.pallas import tpu as pltpu
from jax.sharding import PartitionSpec as P

epsilon = 1e-06
MESH = pl.DeviceIdType.MESH


def block_kernel(
    video_hbm, wt_hbm, bt, wd_hbm, bd, ws_hbm, bs, gain, wq_hbm, wk_hbm, wv_hbm, wo_hbm, y_ref,
    wt, wd, ws, wq, wk, wv, wo, video, lifted, left_of, middle, right_of,
    edges, halo, spatial, held, done,
    load_sem, trade_send, trade_recv, up_send, up_recv, down_send, down_recv, edge_send, edge_recv,
    send_sem, recv_sem, back_sem, home_sem,
):
    frames, height, strip, channels = video_hbm.shape
    halves, _, chunks, groups, pixels, _ = y_ref.shape
    owners, ours = 2 * groups, 2 * halves
    total = groups * ours
    rows = total * pixels
    half = height // 2
    lines = half // chunks
    padded = edges.shape[3]
    me, col, cols = lax.axis_index("tm"), lax.axis_index("cols"), lax.axis_size("cols")
    group, part = lax.div(me, 2), lax.rem(me, 2)
    f32, bf16 = jnp.float32, jnp.bfloat16
    deep = half + 2
    starts = [0] + [lines * (b + 1) + 2 for b in range(chunks)]
    cuts = starts[:-1] + [half + 1]
    offset = 1 - part

    loads = [
        pltpu.make_async_copy(source, target, load_sem.at[i])
        for i, (source, target) in enumerate(
            (
                (
                    video_hbm.at[:, pl.ds((half - 1) * part, half + 1)],
                    video.at[pl.ds(2 + frames * part, frames), pl.ds(offset, half + 1)],
                ),
                (wt_hbm, wt), (wd_hbm, wd), (ws_hbm, ws),
                (wq_hbm, wq), (wk_hbm, wk), (wv_hbm, wv), (wo_hbm, wo),
            )
        )
    ]
    for load in loads:
        load.start()

    barrier = pltpu.get_barrier_semaphore()

    def greet(k, _):
        peer = lax.rem(me + k, owners)
        pl.semaphore_signal(barrier, inc=1, device_id={"tm": peer}, device_id_type=MESH)
        return 0

    lax.fori_loop(1, owners, greet, 0)

    def greet_side(k, _):
        peer = lax.rem(col + k, cols)
        pl.semaphore_signal(barrier, inc=1, device_id={"cols": peer}, device_id_type=MESH)
        return 0

    lax.fori_loop(1, cols, greet_side, 0)

    upper, lower = part == 0, part == 1
    has_next, has_before = group < groups - 1, group > 0
    starts_clip = group == 0
    slots = video.shape[0]
    for part_of, line in ((upper, 0), (lower, deep - 1)):
        @pl.when(part_of)
        def _():
            video[:, line] = jnp.zeros((slots, strip, channels), bf16)

    @pl.when(starts_clip)
    def _():
        video[0:2] = jnp.zeros((2, deep, strip, channels), bf16)
        lifted[0] = jnp.zeros((deep, strip, channels), bf16)

    @pl.when(jnp.logical_not(has_next))
    def _():
        video[slots - 2 :] = jnp.zeros((2, deep, strip, channels), bf16)

    pl.semaphore_wait(barrier, owners + cols - 2)

    def remote(source, target, sent, landed, peer):
        return pltpu.make_async_remote_copy(
            src_ref=source, dst_ref=target, send_sem=sent, recv_sem=landed,
            device_id={"tm": peer}, device_id_type=MESH,
        )

    def trade(i, b):
        first, count = ((frames - 2) * part, 2) if i == 0 else (2 * (1 - part), frames - 2)
        size = cuts[b + 1] - cuts[b]
        return remote(
            video_hbm.at[pl.ds(first, count), pl.ds((half - 1) * (1 - part) + cuts[b], size)],
            video.at[pl.ds(2 + frames * part + first, count), pl.ds(part + cuts[b], size)],
            trade_send.at[i, b], trade_recv.at[i, b], me + 1 - 2 * part,
        )

    def upward(b):
        size = pl.ds(offset + cuts[b], cuts[b + 1] - cuts[b])
        peer = lax.rem(me + 2, owners)
        return remote(video.at[2 * frames + 1, size], video.at[1, size], up_send.at[b], up_recv.at[b], peer)

    def downward(b):
        size = pl.ds(offset + cuts[b], cuts[b + 1] - cuts[b])
        peer = lax.rem(me + owners - 2, owners)
        return remote(
            video.at[pl.ds(2, 2), size], video.at[pl.ds(slots - 2, 2), size],
            down_send.at[b], down_recv.at[b], peer,
        )

    def send_up(b):
        @pl.when(has_next)
        def _():
            upward(b).start()

    def send_down(b):
        @pl.when(has_before)
        def _():
            downward(b).start()

    def pass_on(b):
        trade(0, b).wait_recv()

        @pl.when(upper)
        def _():
            send_up(b)

        @pl.when(lower)
        def _():
            send_down(b)

    def stacked(ref, which, b):
        size = (starts[b + 1] - starts[b]) * strip
        return jnp.concatenate(
            [ref[f, starts[b] : starts[b + 1]].reshape(size, channels) for f in which], 0
        )

    def lift(which, b):
        count = starts[b + 1] - starts[b]
        size = count * strip
        own = [f + 2 for f in which]
        summed = jnp.dot(stacked(video, own, b), wt[0], preferred_element_type=f32)
        for k in (1, 2):
            summed = summed + jnp.dot(
                stacked(video, [f - k for f in own], b), wt[k], preferred_element_type=f32
            )
        summed = summed + bt[...]
        result = (stacked(video, own, b).astype(f32) + jax.nn.silu(summed)).astype(bf16)
        for i, f in enumerate(which):
            lifted[f + 1, starts[b] : starts[b + 1]] = result[i * size : (i + 1) * size].reshape(
                count, strip, channels
            )

    def sideways(low, b, side):
        peer = lax.rem(col + 1, cols) if side == 0 else lax.rem(col + cols - 1, cols)
        which = pl.ds(low, ours + 1 - low)
        return pltpu.make_async_remote_copy(
            src_ref=edges.at[b, side, which], dst_ref=halo.at[b, side, which],
            send_sem=edge_send.at[b, side], recv_sem=edge_recv.at[b, side],
            device_id={"cols": peer}, device_id_type=MESH,
        )

    sends_side = (col < cols - 1, col > 0)
    takes_side = (col > 0, col < cols - 1)

    def reduce_band(low, b):
        first, last = starts[b], starts[b + 1]
        count, many = last - first, ours + 1 - low
        which = range(low, ours + 1)
        summed = jnp.zeros((many * count * strip, channels), f32) + bd[...]
        for k in range(3):
            summed = summed + jnp.dot(
                stacked(lifted, [2 * j + 2 - k for j in which], b), wd[k], preferred_element_type=f32
            )
        middle[low:, first:last] = summed.astype(bf16).reshape(many, count, strip, channels)
        if b == 0:
            @pl.when(upper)
            def _():
                middle[low:, 0] = jnp.zeros((many, strip, channels), bf16)
        if b == chunks - 1:
            @pl.when(lower)
            def _():
                middle[low:, deep - 1] = jnp.zeros((many, strip, channels), bf16)
        wide = middle[low:, first:last].astype(f32)
        rest = jnp.zeros((many, padded - count, channels), f32)
        for side, place in ((0, strip - 1), (1, 0)):
            column = wide[:, :, place]
            column = jnp.concatenate([column, rest], 1) if padded > count else column
            edges[b, side, low:] = column.astype(bf16)
        for side in range(2):
            @pl.when(sends_side[side])
            def _():
                sideways(low, b, side).start()

    def shift_band(low, b):
        first, last = starts[b], starts[b + 1]
        count, many = last - first, ours + 1 - low
        size = many * count * strip
        for side in range(2):
            @pl.when(takes_side[side])
            def _():
                sideways(low, b, side).wait_recv()

            @pl.when(jnp.logical_not(takes_side[side]))
            def _():
                halo[b, side, low:] = jnp.zeros((many, padded, channels), bf16)

        wide = middle[low:, first:last].reshape(size, channels).astype(f32)
        place = lax.rem(lax.broadcasted_iota(jnp.int32, (size, channels), 0), strip)

        def spread(side):
            column = halo[b, side, low:].astype(f32)[:, :count]
            column = jnp.broadcast_to(column[:, :, None, :], (many, count, strip, channels))
            return column.reshape(size, channels)

        before = jnp.where(place == 0, spread(0), pltpu.roll(wide, 1, 0))
        after = jnp.where(place == strip - 1, spread(1), pltpu.roll(wide, size - 1, 0))
        left_of[low:, first:last] = before.astype(bf16).reshape(many, count, strip, channels)
        right_of[low:, first:last] = after.astype(bf16).reshape(many, count, strip, channels)

    def convolve_band(low, c):
        first, many = c * lines, ours + 1 - low

        def window(ref, a):
            return ref[low:, first + a : first + a + lines].reshape(many * lines * strip, channels)

        summed = jnp.zeros((many * lines * strip, channels), f32) + bs[...]
        for k, shifted in ((1, middle), (0, left_of), (2, right_of)):
            for a in range(3):
                summed = summed + jnp.dot(
                    window(shifted, a), ws[3 * a + k], preferred_element_type=f32
                )
        result = (window(middle, 1).astype(f32) + jax.nn.silu(summed)).astype(bf16)
        result = result.reshape(many, groups, pixels, channels)
        for j in range(many):
            spatial[c, :, low + j] = result[j]

    def by_group(which, act):
        @pl.when(which == 0)
        def _():
            act(0, ours + 1)

        @pl.when((which > 0) & (which < groups - 1))
        def _():
            act(1, ours)

        @pl.when(which == groups - 1)
        def _():
            act(1, ours - 1)

    def outward(low, count, c, peer, slot, source):
        first = ours * source + 1 if low else 0
        return remote(
            spatial.at[c, peer, pl.ds(low, count)], held.at[c, pl.ds(first, count)],
            send_sem.at[c, slot], recv_sem.at[c, source], 2 * peer + part,
        )

    def homeward(c, peer, slot, source, side, line):
        return remote(
            done.at[c, peer], y_ref.at[:, side, c, line], back_sem.at[c, slot], home_sem.at[c, source], peer
        )

    def scatter(c):
        def act(low, count):
            def send(k, _):
                outward(low, count, c, lax.rem(group + k, groups), k, group).start()
                return 0

            lax.fori_loop(1, groups, send, 0)

        by_group(group, act)

    def attend(c):
        def keep(low, count):
            first = ours * group + 1 if low else 0
            held[c, pl.ds(first, count)] = spatial[c, group, low : low + count]

        by_group(group, keep)

        def arrive(k, _):
            source = lax.rem(group + groups - k, groups)

            def act(low, count):
                outward(low, count, c, lax.rem(group + k, groups), k, source).wait_recv()

            by_group(source, act)
            return 0

        lax.fori_loop(1, groups, arrive, 0)
        place = lax.broadcasted_iota(jnp.int32, (rows, rows), 0)
        other = lax.broadcasted_iota(jnp.int32, (rows, rows), 1)
        allowed = (lax.rem(place, pixels) == lax.rem(other, pixels)) & (other <= place)
        wide = held[c].reshape(rows, channels).astype(f32)
        scale = lax.rsqrt(jnp.mean(wide * wide, axis=-1, keepdims=True) + epsilon)
        normed = (wide * scale * gain[...]).astype(bf16)
        query = jnp.dot(normed, wq[...], preferred_element_type=f32).astype(bf16)
        key = jnp.dot(normed, wk[...], preferred_element_type=f32).astype(bf16)
        value = jnp.dot(normed, wv[...], preferred_element_type=f32).astype(bf16)
        scores = lax.dot_general(
            query, key, (((1,), (1,)), ((), ())), preferred_element_type=f32
        ) * channels ** (-0.5)
        scores = jnp.where(allowed, scores, -1e30)
        largest = jnp.max(scores, axis=-1, keepdims=True)
        probs = jnp.exp(scores - largest)
        probs = (probs / jnp.sum(probs, axis=-1, keepdims=True)).astype(bf16)
        context = jnp.dot(probs, value, preferred_element_type=f32).astype(bf16)
        mixed = jnp.dot(context, wo[...], preferred_element_type=f32)
        result = (wide + mixed).astype(bf16)
        done[c] = result.reshape(owners, halves, pixels, channels)

        def back(k, _):
            homeward(c, lax.rem(me + k, owners), k, me, part, group).start()
            return 0

        lax.fori_loop(1, owners, back, 0)
        y_ref[:, part, c, group] = done[c, me]

    for b in range(chunks):
        for i in range(2):
            trade(i, b).start()
    loads[0].wait()
    for b in range(chunks):
        @pl.when(lower)
        def _():
            send_up(b)

        @pl.when(upper)
        def _():
            send_down(b)
    for load in loads[1:]:
        load.wait()

    last = 2 * frames
    pass_on(0)
    for b in range(chunks):
        trade(1, b).wait_recv()

        def band(low):
            lift(range(2 * low, last), b)
            if low:
                upward(b).wait_recv()

            @pl.when(has_next)
            def _():
                downward(b).wait_recv()

            lift(([1] if low else []) + [last, last + 1], b)
            reduce_band(low, b)
            if b + 1 < chunks:
                pass_on(b + 1)
            shift_band(low, b)
            convolve_band(low, b)

        @pl.when(starts_clip)
        def _():
            band(0)

        @pl.when(has_before)
        def _():
            band(1)

        scatter(b)
    for c in range(chunks):
        attend(c)

    for b in range(chunks):
        for i in range(2):
            trade(i, b).wait_send()

        @pl.when(has_next)
        def _():
            upward(b).wait_send()

        @pl.when(has_before)
        def _():
            downward(b).wait_send()

        for low, chosen in ((0, starts_clip), (1, has_before)):
            for side in range(2):
                @pl.when(sends_side[side] & chosen)
                def _():
                    sideways(low, b, side).wait_send()

    for c in range(chunks):
        def left(low, count):
            def sent(k, _):
                outward(low, count, c, lax.rem(group + k, groups), k, group).wait_send()
                return 0

            lax.fori_loop(1, groups, sent, 0)

        by_group(group, left)

        def finish(k, _):
            peer, source = lax.rem(me + k, owners), lax.rem(me + owners - k, owners)
            homeward(c, peer, k, me, part, group).wait_send()
            homeward(c, peer, k, source, lax.rem(source, 2), lax.div(source, 2)).wait_recv()
            return 0

        lax.fori_loop(1, owners, finish, 0)


def per_device(
    video, w_time, b_time, w_down, b_down, w_space, b_space, gain, w_query, w_key, w_value, w_out
):
    frames, height, strip, channels = video.shape
    halves, owners = frames // 2, lax.axis_size("tm")
    groups, half = owners // 2, height // 2
    owned = half * strip // groups
    pixels = min(16, owned)
    chunks = owned // pixels
    deep, slots = half + 2, 2 * halves + 1
    padded = -(-(half // chunks + 2) // 8) * 8
    vmem = pl.BlockSpec(memory_space=pltpu.VMEM)
    hbm = pl.BlockSpec(memory_space=pltpu.HBM)
    bf16 = jnp.bfloat16
    square = (channels, channels)
    shifted = pltpu.VMEM((slots, deep, strip, channels), bf16)
    flat = lambda v: v.reshape(1, channels)
    sems = pltpu.SemaphoreType.DMA
    result = pl.pallas_call(
        block_kernel,
        out_shape=jax.ShapeDtypeStruct((halves, 2, chunks, groups, pixels, channels), bf16),
        in_specs=[hbm, hbm, vmem, hbm, vmem, hbm, vmem, vmem, hbm, hbm, hbm, hbm],
        out_specs=vmem,
        scratch_shapes=[
            pltpu.VMEM((3,) + square, bf16),
            pltpu.VMEM((3,) + square, bf16),
            pltpu.VMEM((9,) + square, bf16),
            pltpu.VMEM(square, bf16),
            pltpu.VMEM(square, bf16),
            pltpu.VMEM(square, bf16),
            pltpu.VMEM(square, bf16),
            pltpu.VMEM((2 * frames + 4, deep, strip, channels), bf16),
            pltpu.VMEM((2 * frames + 3, deep, strip, channels), bf16),
            shifted,
            shifted,
            shifted,
            pltpu.VMEM((chunks, 2, slots, padded, channels), bf16),
            pltpu.VMEM((chunks, 2, slots, padded, channels), bf16),
            pltpu.VMEM((chunks, groups, slots, pixels, channels), bf16),
            pltpu.VMEM((chunks, owners * halves, pixels, channels), bf16),
            pltpu.VMEM((chunks, owners, halves, pixels, channels), bf16),
            sems((8,)),
            sems((2, chunks)),
            sems((2, chunks)),
            sems((chunks,)),
            sems((chunks,)),
            sems((chunks,)),
            sems((chunks,)),
            sems((chunks, 2)),
            sems((chunks, 2)),
            sems((chunks, groups)),
            sems((chunks, groups)),
            sems((chunks, owners)),
            sems((chunks, owners)),
        ],
        compiler_params=pltpu.CompilerParams(
            collective_id=0, has_side_effects=True, vmem_limit_bytes=57 * 1024 * 1024
        ),
    )(
        video, w_time, flat(b_time), w_down, flat(b_down),
        w_space, flat(b_space), flat(gain), w_query, w_key, w_value, w_out,
    )
    return result.reshape(halves, height, strip, channels)


def solution(mesh):
    return jax.shard_map(
        per_device,
        mesh=mesh,
        in_specs=(P(("clips", "tm"), None, "cols", None),) + (P(),) * 11,
        out_specs=P(("clips", "tm"), None, "cols", None),
        check_vma=False,
    )
```

```python
import jax
import jax.numpy as jnp
from jax import lax
from jax.experimental import pallas as pl
from jax.experimental.pallas import tpu as pltpu
from jax.sharding import PartitionSpec as P

epsilon = 1e-06
MESH = pl.DeviceIdType.MESH


def block_kernel(
    video_hbm, wt_hbm, bt, wd_hbm, bd, ws_hbm, bs, gain, wq_hbm, wk_hbm, wv_hbm, wo_hbm, y_ref,
    wt, wd, ws, wq, wk, wv, wo, video, lifted, left_of, middle, right_of,
    edges, halo, spatial, held, done,
    load_sem, trade_send, trade_recv, up_send, up_recv, down_send, down_recv, edge_send, edge_recv,
    send_sem, recv_sem, tail_send, tail_recv, head_send, head_recv, back_sem, home_sem,
):
    frames, height, strip, channels = video_hbm.shape
    halves, _, chunks, groups, pixels, _ = y_ref.shape
    owners, ours = 2 * groups, 2 * halves
    total = groups * ours
    rows = total * pixels
    half = height // 2
    lines = half // chunks
    padded = edges.shape[3]
    joint = 2 if chunks % 2 == 0 else 1
    me, col, cols = lax.axis_index("tm"), lax.axis_index("cols"), lax.axis_size("cols")
    group, part = lax.div(me, 2), lax.rem(me, 2)
    f32, bf16 = jnp.float32, jnp.bfloat16
    deep = half + 2
    starts = [0] + [lines * (b + 1) + 2 for b in range(chunks)]
    cuts = starts[:-1] + [half + 1]
    offset = 1 - part

    loads = [
        pltpu.make_async_copy(source, target, load_sem.at[i])
        for i, (source, target) in enumerate(
            (
                (
                    video_hbm.at[:, pl.ds((half - 1) * part, half + 1)],
                    video.at[pl.ds(2 + frames * part, frames), pl.ds(offset, half + 1)],
                ),
                (wt_hbm, wt), (wd_hbm, wd), (ws_hbm, ws),
                (wq_hbm, wq), (wk_hbm, wk), (wv_hbm, wv), (wo_hbm, wo),
            )
        )
    ]
    for load in loads:
        load.start()

    barrier = pltpu.get_barrier_semaphore()

    def greet(k, _):
        peer = lax.rem(me + k, owners)
        pl.semaphore_signal(barrier, inc=1, device_id={"tm": peer}, device_id_type=MESH)
        return 0

    lax.fori_loop(1, owners, greet, 0)

    def greet_side(k, _):
        peer = lax.rem(col + k, cols)
        pl.semaphore_signal(barrier, inc=1, device_id={"cols": peer}, device_id_type=MESH)
        return 0

    lax.fori_loop(1, cols, greet_side, 0)

    upper, lower = part == 0, part == 1
    has_next, has_before = group < groups - 1, group > 0
    starts_clip = group == 0
    slots = video.shape[0]
    for part_of, line in ((upper, 0), (lower, deep - 1)):
        @pl.when(part_of)
        def _():
            video[:, line] = jnp.zeros((slots, strip, channels), bf16)

    @pl.when(starts_clip)
    def _():
        video[0:2] = jnp.zeros((2, deep, strip, channels), bf16)
        lifted[0] = jnp.zeros((deep, strip, channels), bf16)

    @pl.when(jnp.logical_not(has_next))
    def _():
        video[slots - 2 :] = jnp.zeros((2, deep, strip, channels), bf16)

    pl.semaphore_wait(barrier, owners + cols - 2)

    def remote(source, target, sent, landed, peer):
        return pltpu.make_async_remote_copy(
            src_ref=source, dst_ref=target, send_sem=sent, recv_sem=landed,
            device_id={"tm": peer}, device_id_type=MESH,
        )

    def trade(i, b):
        first, count = ((frames - 2) * part, 2) if i == 0 else (2 * (1 - part), frames - 2)
        size = cuts[b + 1] - cuts[b]
        return remote(
            video_hbm.at[pl.ds(first, count), pl.ds((half - 1) * (1 - part) + cuts[b], size)],
            video.at[pl.ds(2 + frames * part + first, count), pl.ds(part + cuts[b], size)],
            trade_send.at[i, b], trade_recv.at[i, b], me + 1 - 2 * part,
        )

    def upward(b):
        size = pl.ds(offset + cuts[b], cuts[b + 1] - cuts[b])
        peer = lax.rem(me + 2, owners)
        return remote(video.at[2 * frames + 1, size], video.at[1, size], up_send.at[b], up_recv.at[b], peer)

    def downward(b):
        size = pl.ds(offset + cuts[b], cuts[b + 1] - cuts[b])
        peer = lax.rem(me + owners - 2, owners)
        return remote(
            video.at[pl.ds(2, 2), size], video.at[pl.ds(slots - 2, 2), size],
            down_send.at[b], down_recv.at[b], peer,
        )

    def send_up(b):
        @pl.when(has_next)
        def _():
            upward(b).start()

    def send_down(b):
        @pl.when(has_before)
        def _():
            downward(b).start()

    def pass_on(b):
        trade(0, b).wait_recv()

        @pl.when(upper)
        def _():
            send_up(b)

        @pl.when(lower)
        def _():
            send_down(b)

    def stacked(ref, which, first, last):
        size = (last - first) * strip
        return jnp.concatenate([ref[f, first:last].reshape(size, channels) for f in which], 0)

    def lift(which, first, last):
        count = last - first
        size = count * strip
        own = [f + 2 for f in which]
        summed = jnp.dot(stacked(video, own, first, last), wt[0], preferred_element_type=f32)
        for k in (1, 2):
            summed = summed + jnp.dot(
                stacked(video, [f - k for f in own], first, last), wt[k], preferred_element_type=f32
            )
        summed = summed + bt[...]
        result = (stacked(video, own, first, last).astype(f32) + jax.nn.silu(summed)).astype(bf16)
        for i, f in enumerate(which):
            lifted[f + 1, first:last] = result[i * size : (i + 1) * size].reshape(count, strip, channels)

    def sideways(step, many, side):
        peer = lax.rem(col + 1, cols) if side == 0 else lax.rem(col + cols - 1, cols)
        which = pl.ds(0, many)
        return pltpu.make_async_remote_copy(
            src_ref=edges.at[step, side, which], dst_ref=halo.at[step, side, which],
            send_sem=edge_send.at[step, side], recv_sem=edge_recv.at[step, side],
            device_id={"cols": peer}, device_id_type=MESH,
        )

    sends_side = (col < cols - 1, col > 0)
    takes_side = (col > 0, col < cols - 1)

    def reduce_rows(step, which, first, last):
        count, many = last - first, len(which)
        size = count * strip
        summed = jnp.zeros((many * size, channels), f32) + bd[...]
        for k in range(3):
            summed = summed + jnp.dot(
                stacked(lifted, [2 * j + 2 - k for j in which], first, last), wd[k],
                preferred_element_type=f32,
            )
        reduced = summed.astype(bf16)
        for i, j in enumerate(which):
            middle[j, first:last] = reduced[i * size : (i + 1) * size].reshape(count, strip, channels)
            for chosen, line in ((upper, 0), (lower, deep - 1)):
                if first <= line < last:
                    @pl.when(chosen)
                    def _():
                        middle[j, line] = jnp.zeros((strip, channels), bf16)
        wide = stacked(middle, which, first, last).astype(f32).reshape(many, count, strip, channels)
        rest = jnp.zeros((many, padded - count, channels), f32)
        for side, place in ((0, strip - 1), (1, 0)):
            column = wide[:, :, place]
            column = jnp.concatenate([column, rest], 1) if padded > count else column
            edges[step, side, :many] = column.astype(bf16)
        for side in range(2):
            @pl.when(sends_side[side])
            def _():
                sideways(step, many, side).start()

    def shift_rows(step, which, first, last):
        count, many = last - first, len(which)
        part_size = count * strip
        size = many * part_size
        for side in range(2):
            @pl.when(takes_side[side])
            def _():
                sideways(step, many, side).wait_recv()

            @pl.when(jnp.logical_not(takes_side[side]))
            def _():
                halo[step, side, :many] = jnp.zeros((many, padded, channels), bf16)

        wide = stacked(middle, which, first, last).astype(f32)
        place = lax.rem(lax.broadcasted_iota(jnp.int32, (size, channels), 0), strip)

        def spread(side):
            column = halo[step, side, :many].astype(f32)[:, :count]
            column = jnp.broadcast_to(column[:, :, None, :], (many, count, strip, channels))
            return column.reshape(size, channels)

        before = jnp.where(place == 0, spread(0), pltpu.roll(wide, 1, 0)).astype(bf16)
        after = jnp.where(place == strip - 1, spread(1), pltpu.roll(wide, size - 1, 0)).astype(bf16)
        for i, j in enumerate(which):
            own = slice(i * part_size, (i + 1) * part_size)
            left_of[j, first:last] = before[own].reshape(count, strip, channels)
            right_of[j, first:last] = after[own].reshape(count, strip, channels)

    def convolve_chunks(which, first, count):
        top, deep_rows = first * lines, count * lines
        many = len(which)

        def window(ref, a):
            return stacked(ref, which, top + a, top + a + deep_rows)

        summed = jnp.zeros((many * deep_rows * strip, channels), f32) + bs[...]
        for k, shifted in ((1, middle), (0, left_of), (2, right_of)):
            for a in range(3):
                summed = summed + jnp.dot(
                    window(shifted, a), ws[3 * a + k], preferred_element_type=f32
                )
        result = (window(middle, 1).astype(f32) + jax.nn.silu(summed)).astype(bf16)
        result = result.reshape(many, count, groups, pixels, channels)
        for i, j in enumerate(which):
            for c in range(count):
                spatial[first + c, :, j] = result[i, c]

    def outward(c, peer, slot, source):
        count = ours - 1
        return remote(
            spatial.at[c, peer, pl.ds(1, count)], held.at[c, pl.ds(ours * source + 1, count)],
            send_sem.at[c, slot], recv_sem.at[c, source], 2 * peer + part,
        )

    def tailward(c, peer, slot, source):
        frame = lax.rem(ours * (source + 1), total)
        return remote(
            spatial.at[c, peer, ours], held.at[c, frame],
            tail_send.at[c, slot], tail_recv.at[c, source], 2 * peer + part,
        )

    def headward(c, peer, slot):
        return remote(
            spatial.at[c, peer, 0], held.at[c, 0], head_send.at[c, slot], head_recv.at[c], 2 * peer + part
        )

    def homeward(c, peer, slot, source, side, line):
        return remote(
            done.at[c, peer], y_ref.at[:, side, c, line], back_sem.at[c, slot], home_sem.at[c, source], peer
        )

    def others(act):
        def step(k, _):
            act(k, lax.rem(group + k, groups), lax.rem(group + groups - k, groups))
            return 0

        lax.fori_loop(1, groups, step, 0)

    def scatter(c):
        others(lambda k, peer, source: outward(c, peer, k, group).start())

    def scatter_late(c):
        @pl.when(has_next)
        def _():
            others(lambda k, peer, source: tailward(c, peer, k, group).start())

        @pl.when(starts_clip)
        def _():
            others(lambda k, peer, source: headward(c, peer, k).start())

    def attend(c):
        held[c, pl.ds(ours * group + 1, ours - 1)] = spatial[c, group, 1:ours]

        @pl.when(has_next)
        def _():
            held[c, ours * group + ours] = spatial[c, group, ours]

        @pl.when(starts_clip)
        def _():
            held[c, 0] = spatial[c, group, 0]

        def arrive(k, peer, source):
            outward(c, peer, k, source).wait_recv()

            @pl.when(source < groups - 1)
            def _():
                tailward(c, peer, k, source).wait_recv()

        others(arrive)

        @pl.when(has_before)
        def _():
            headward(c, 0, 0).wait_recv()

        place = lax.broadcasted_iota(jnp.int32, (rows, rows), 0)
        other = lax.broadcasted_iota(jnp.int32, (rows, rows), 1)
        allowed = (lax.rem(place, pixels) == lax.rem(other, pixels)) & (other <= place)
        wide = held[c].reshape(rows, channels).astype(f32)
        scale = lax.rsqrt(jnp.mean(wide * wide, axis=-1, keepdims=True) + epsilon)
        normed = (wide * scale * gain[...]).astype(bf16)
        query = jnp.dot(normed, wq[...], preferred_element_type=f32).astype(bf16)
        key = jnp.dot(normed, wk[...], preferred_element_type=f32).astype(bf16)
        value = jnp.dot(normed, wv[...], preferred_element_type=f32).astype(bf16)
        scores = lax.dot_general(
            query, key, (((1,), (1,)), ((), ())), preferred_element_type=f32
        ) * channels ** (-0.5)
        scores = jnp.where(allowed, scores, -1e30)
        largest = jnp.max(scores, axis=-1, keepdims=True)
        probs = jnp.exp(scores - largest)
        probs = (probs / jnp.sum(probs, axis=-1, keepdims=True)).astype(bf16)
        context = jnp.dot(probs, value, preferred_element_type=f32).astype(bf16)
        mixed = jnp.dot(context, wo[...], preferred_element_type=f32)
        result = (wide + mixed).astype(bf16)
        done[c] = result.reshape(owners, halves, pixels, channels)

        def back(k, _):
            homeward(c, lax.rem(me + k, owners), k, me, part, group).start()
            return 0

        lax.fori_loop(1, owners, back, 0)
        y_ref[:, part, c, group] = done[c, me]

    for b in range(chunks):
        for i in range(2):
            trade(i, b).start()
    loads[0].wait()
    for b in range(chunks):
        @pl.when(lower)
        def _():
            send_up(b)

        @pl.when(upper)
        def _():
            send_down(b)
    for load in loads[1:]:
        load.wait()

    final = 2 * frames
    main, ends = tuple(range(1, ours)), (0, ours)
    steps = chunks + chunks // joint

    def late(step, which, lifts, first):
        span = starts[first], starts[first + joint]
        lift(lifts, *span)
        reduce_rows(step, which, *span)
        shift_rows(step, which, *span)
        convolve_chunks(which, first, joint)

    pass_on(0)
    for b in range(chunks):
        trade(1, b).wait_recv()

        @pl.when(has_before)
        def _():
            upward(b).wait_recv()

        lift(range(1, final), starts[b], starts[b + 1])
        reduce_rows(b, main, starts[b], starts[b + 1])
        shift_rows(b, main, starts[b], starts[b + 1])
        convolve_chunks(main, b, 1)
        if b + 1 < chunks:
            pass_on(b + 1)
        scatter(b)
        if (b + 1) % joint == 0:
            first = b + 1 - joint
            step = chunks + first // joint

            @pl.when(has_next)
            def _():
                for d in range(first, first + joint):
                    downward(d).wait_recv()

            @pl.when(starts_clip)
            def _():
                late(step, ends, (0, final, final + 1), first)

            @pl.when(has_before & has_next)
            def _():
                late(step, ends[1:], (final, final + 1), first)

            for c in range(first, first + joint):
                scatter_late(c)
    for c in range(chunks):
        attend(c)

    for b in range(chunks):
        for i in range(2):
            trade(i, b).wait_send()

        @pl.when(has_next)
        def _():
            upward(b).wait_send()

        @pl.when(has_before)
        def _():
            downward(b).wait_send()

    for step in range(steps):
        kinds = ((len(main), col >= 0),)
        if step >= chunks:
            kinds = ((2, starts_clip), (1, has_before & has_next))
        for many, chosen in kinds:
            for side in range(2):
                @pl.when(sends_side[side] & chosen)
                def _():
                    sideways(step, many, side).wait_send()

    for c in range(chunks):
        others(lambda k, peer, source: outward(c, peer, k, group).wait_send())

        @pl.when(has_next)
        def _():
            others(lambda k, peer, source: tailward(c, peer, k, group).wait_send())

        @pl.when(starts_clip)
        def _():
            others(lambda k, peer, source: headward(c, peer, k).wait_send())

        def finish(k, _):
            peer, source = lax.rem(me + k, owners), lax.rem(me + owners - k, owners)
            homeward(c, peer, k, me, part, group).wait_send()
            homeward(c, peer, k, source, lax.rem(source, 2), lax.div(source, 2)).wait_recv()
            return 0

        lax.fori_loop(1, owners, finish, 0)


def per_device(
    video, w_time, b_time, w_down, b_down, w_space, b_space, gain, w_query, w_key, w_value, w_out
):
    frames, height, strip, channels = video.shape
    halves, owners = frames // 2, lax.axis_size("tm")
    groups, half = owners // 2, height // 2
    owned = half * strip // groups
    pixels = min(16, owned)
    chunks = owned // pixels
    deep, slots = half + 2, 2 * halves + 1
    joint = 2 if chunks % 2 == 0 else 1
    padded = -(-(joint * half // chunks + 2) // 8) * 8
    steps = chunks + chunks // joint
    vmem = pl.BlockSpec(memory_space=pltpu.VMEM)
    hbm = pl.BlockSpec(memory_space=pltpu.HBM)
    bf16 = jnp.bfloat16
    square = (channels, channels)
    shifted = pltpu.VMEM((slots, deep, strip, channels), bf16)
    flat = lambda v: v.reshape(1, channels)
    sems = pltpu.SemaphoreType.DMA
    result = pl.pallas_call(
        block_kernel,
        out_shape=jax.ShapeDtypeStruct((halves, 2, chunks, groups, pixels, channels), bf16),
        in_specs=[hbm, hbm, vmem, hbm, vmem, hbm, vmem, vmem, hbm, hbm, hbm, hbm],
        out_specs=vmem,
        scratch_shapes=[
            pltpu.VMEM((3,) + square, bf16),
            pltpu.VMEM((3,) + square, bf16),
            pltpu.VMEM((9,) + square, bf16),
            pltpu.VMEM(square, bf16),
            pltpu.VMEM(square, bf16),
            pltpu.VMEM(square, bf16),
            pltpu.VMEM(square, bf16),
            pltpu.VMEM((2 * frames + 4, deep, strip, channels), bf16),
            pltpu.VMEM((2 * frames + 3, deep, strip, channels), bf16),
            shifted,
            shifted,
            shifted,
            pltpu.VMEM((steps, 2, slots, padded, channels), bf16),
            pltpu.VMEM((steps, 2, slots, padded, channels), bf16),
            pltpu.VMEM((chunks, groups, slots, pixels, channels), bf16),
            pltpu.VMEM((chunks, owners * halves, pixels, channels), bf16),
            pltpu.VMEM((chunks, owners, halves, pixels, channels), bf16),
            sems((8,)),
            sems((2, chunks)),
            sems((2, chunks)),
            sems((chunks,)),
            sems((chunks,)),
            sems((chunks,)),
            sems((chunks,)),
            sems((steps, 2)),
            sems((steps, 2)),
            sems((chunks, groups)),
            sems((chunks, groups)),
            sems((chunks, groups)),
            sems((chunks, groups)),
            sems((chunks, groups)),
            sems((chunks,)),
            sems((chunks, owners)),
            sems((chunks, owners)),
        ],
        compiler_params=pltpu.CompilerParams(
            collective_id=0, has_side_effects=True, vmem_limit_bytes=57 * 1024 * 1024
        ),
    )(
        video, w_time, flat(b_time), w_down, flat(b_down),
        w_space, flat(b_space), flat(gain), w_query, w_key, w_value, w_out,
    )
    return result.reshape(halves, height, strip, channels)


def solution(mesh):
    return jax.shard_map(
        per_device,
        mesh=mesh,
        in_specs=(P(("clips", "tm"), None, "cols", None),) + (P(),) * 11,
        out_specs=P(("clips", "tm"), None, "cols", None),
        check_vma=False,
    )
```

```python
import jax
import jax.numpy as jnp
from jax import lax
from jax.experimental import pallas as pl
from jax.experimental.pallas import tpu as pltpu
from jax.sharding import PartitionSpec as P

epsilon = 1e-06
MESH = pl.DeviceIdType.MESH


def block_kernel(
    video_hbm, wt_hbm, bt, wd_hbm, bd, ws_hbm, bs, gain, wq_hbm, wk_hbm, wv_hbm, wo_hbm, y_ref,
    wt, wd, ws, wq, wk, wv, wo, video, lifted, left_of, middle, right_of,
    edges, halo, spatial, held, done,
    load_sem, trade_send, trade_recv, up_send, up_recv, down_send, down_recv, edge_send, edge_recv,
    send_sem, recv_sem, tail_send, tail_recv, head_send, head_recv, back_sem, home_sem,
    from_below, from_above, from_partner,
):
    frames, height, strip, channels = video_hbm.shape
    _, chunks, groups, halves, pixels, _ = y_ref.shape
    owners, ours = 2 * groups, 2 * halves
    total = groups * ours
    rows = total * pixels
    half = height // 2
    lines = half // chunks
    padded = edges.shape[3]
    joint = 2 if chunks % 2 == 0 else 1
    me, col, cols = lax.axis_index("tm"), lax.axis_index("cols"), lax.axis_size("cols")
    group, part = lax.div(me, 2), lax.rem(me, 2)
    f32, bf16 = jnp.float32, jnp.bfloat16
    deep = half + 2
    starts = [0] + [lines * (b + 1) + 2 for b in range(chunks)]
    cuts = starts[:-1] + [half + 1]
    offset = 1 - part
    lead = min(1, chunks)

    loads = [
        pltpu.make_async_copy(source, target, load_sem.at[i])
        for i, (source, target) in enumerate(
            (
                (
                    video_hbm.at[:, pl.ds((half - 1) * part, half + 1)],
                    video.at[pl.ds(2 + frames * part, frames), pl.ds(offset, half + 1)],
                ),
                (wt_hbm, wt), (wd_hbm, wd), (ws_hbm, ws),
                (wq_hbm, wq), (wk_hbm, wk), (wv_hbm, wv), (wo_hbm, wo),
            )
        )
    ]
    for load in loads:
        load.start()

    barrier = pltpu.get_barrier_semaphore()

    upper, lower = part == 0, part == 1
    has_next, has_before = group < groups - 1, group > 0

    def tell(semaphore, peer):
        pl.semaphore_signal(semaphore, inc=1, device_id={"tm": peer}, device_id_type=MESH)

    partner = me + 1 - 2 * part
    above, below = lax.rem(me + 2, owners), lax.rem(me + owners - 2, owners)
    tell(barrier, partner)

    @pl.when(has_next)
    def _():
        tell(barrier, above)

    @pl.when(has_before)
    def _():
        tell(barrier, below)

    def greet_side(k, _):
        peer = lax.rem(col + k, cols)
        pl.semaphore_signal(barrier, inc=1, device_id={"cols": peer}, device_id_type=MESH)
        return 0

    lax.fori_loop(1, cols, greet_side, 0)

    starts_clip = group == 0
    slots = video.shape[0]
    for part_of, line in ((upper, 0), (lower, deep - 1)):
        @pl.when(part_of)
        def _():
            video[:, line] = jnp.zeros((slots, strip, channels), bf16)

    @pl.when(starts_clip)
    def _():
        video[0:2] = jnp.zeros((2, deep, strip, channels), bf16)
        lifted[0] = jnp.zeros((deep, strip, channels), bf16)

    @pl.when(jnp.logical_not(has_next))
    def _():
        video[slots - 2 :] = jnp.zeros((2, deep, strip, channels), bf16)

    pl.semaphore_wait(barrier, cols + jnp.where(has_next, 1, 0) + jnp.where(has_before, 1, 0))

    def remote(source, target, sent, landed, peer):
        return pltpu.make_async_remote_copy(
            src_ref=source, dst_ref=target, send_sem=sent, recv_sem=landed,
            device_id={"tm": peer}, device_id_type=MESH,
        )

    def trade(i, b):
        first, count = (frames - 1, 1) if i == 0 else (0, frames - 1)
        size = cuts[b + 1] - cuts[b]
        return remote(
            video_hbm.at[pl.ds(first, count), pl.ds((half - 1) * (1 - part) + cuts[b], size)],
            video.at[pl.ds(2 + frames * part + first, count), pl.ds(part + cuts[b], size)],
            trade_send.at[i, b], trade_recv.at[i, b], me + 1 - 2 * part,
        )

    def upward(b):
        size = pl.ds(offset + cuts[b], cuts[b + 1] - cuts[b])
        peer = lax.rem(me + 2, owners)
        return remote(video.at[2 * frames + 1, size], video.at[1, size], up_send.at[b], up_recv.at[b], peer)

    def downward(b):
        size = pl.ds(offset + cuts[b], cuts[b + 1] - cuts[b])
        peer = lax.rem(me + owners - 2, owners)
        return remote(
            video.at[pl.ds(2, 2), size], video.at[pl.ds(slots - 2, 2), size],
            down_send.at[b], down_recv.at[b], peer,
        )

    def send_up(b):
        @pl.when(has_next)
        def _():
            upward(b).start()

    def send_down(b):
        @pl.when(has_before)
        def _():
            downward(b).start()

    def pass_up(b):
        if b < chunks:
            trade(0, b).wait_recv()

            @pl.when(upper)
            def _():
                send_up(b)

    def pass_down(b):
        @pl.when(lower)
        def _():
            send_down(b)

    def stacked(ref, which, first, last):
        size = (last - first) * strip
        return jnp.concatenate([ref[f, first:last].reshape(size, channels) for f in which], 0)

    def lift(which, first, last):
        count = last - first
        size = count * strip
        own = [f + 2 for f in which]
        summed = jnp.dot(stacked(video, own, first, last), wt[0], preferred_element_type=f32)
        for k in (1, 2):
            summed = summed + jnp.dot(
                stacked(video, [f - k for f in own], first, last), wt[k], preferred_element_type=f32
            )
        summed = summed + bt[...]
        result = (stacked(video, own, first, last).astype(f32) + jax.nn.silu(summed)).astype(bf16)
        for i, f in enumerate(which):
            lifted[f + 1, first:last] = result[i * size : (i + 1) * size].reshape(count, strip, channels)

    def sideways(step, many, side):
        peer = lax.rem(col + 1, cols) if side == 0 else lax.rem(col + cols - 1, cols)
        which = pl.ds(0, many)
        return pltpu.make_async_remote_copy(
            src_ref=edges.at[step, side, which], dst_ref=halo.at[step, side, which],
            send_sem=edge_send.at[step, side], recv_sem=edge_recv.at[step, side],
            device_id={"cols": peer}, device_id_type=MESH,
        )

    sends_side = (col < cols - 1, col > 0)
    takes_side = (col > 0, col < cols - 1)

    def reduce_rows(step, which, first, last):
        count, many = last - first, len(which)
        size = count * strip
        summed = jnp.zeros((many * size, channels), f32) + bd[...]
        for k in range(3):
            summed = summed + jnp.dot(
                stacked(lifted, [2 * j + 2 - k for j in which], first, last), wd[k],
                preferred_element_type=f32,
            )
        reduced = summed.astype(bf16)
        for i, j in enumerate(which):
            middle[j, first:last] = reduced[i * size : (i + 1) * size].reshape(count, strip, channels)
            for chosen, line in ((upper, 0), (lower, deep - 1)):
                if first <= line < last:
                    @pl.when(chosen)
                    def _():
                        middle[j, line] = jnp.zeros((strip, channels), bf16)
        wide = stacked(middle, which, first, last).astype(f32).reshape(many, count, strip, channels)
        rest = jnp.zeros((many, padded - count, channels), f32)
        for side, place in ((0, strip - 1), (1, 0)):
            column = wide[:, :, place]
            column = jnp.concatenate([column, rest], 1) if padded > count else column
            edges[step, side, :many] = column.astype(bf16)
        for side in range(2):
            @pl.when(sends_side[side])
            def _():
                sideways(step, many, side).start()

    def shift_rows(step, which, first, last):
        count, many = last - first, len(which)
        part_size = count * strip
        size = many * part_size
        for side in range(2):
            @pl.when(takes_side[side])
            def _():
                sideways(step, many, side).wait_recv()

            @pl.when(jnp.logical_not(takes_side[side]))
            def _():
                halo[step, side, :many] = jnp.zeros((many, padded, channels), bf16)

        wide = stacked(middle, which, first, last).astype(f32)
        place = lax.rem(lax.broadcasted_iota(jnp.int32, (size, channels), 0), strip)

        def spread(side):
            column = halo[step, side, :many].astype(f32)[:, :count]
            column = jnp.broadcast_to(column[:, :, None, :], (many, count, strip, channels))
            return column.reshape(size, channels)

        before = jnp.where(place == 0, spread(0), pltpu.roll(wide, 1, 0)).astype(bf16)
        after = jnp.where(place == strip - 1, spread(1), pltpu.roll(wide, size - 1, 0)).astype(bf16)
        for i, j in enumerate(which):
            own = slice(i * part_size, (i + 1) * part_size)
            left_of[j, first:last] = before[own].reshape(count, strip, channels)
            right_of[j, first:last] = after[own].reshape(count, strip, channels)

    def convolve_chunks(which, first, count):
        top, deep_rows = first * lines, count * lines
        many = len(which)

        def window(ref, a):
            return stacked(ref, which, top + a, top + a + deep_rows)

        summed = jnp.zeros((many * deep_rows * strip, channels), f32) + bs[...]
        for k, shifted in ((1, middle), (0, left_of), (2, right_of)):
            for a in range(3):
                summed = summed + jnp.dot(
                    window(shifted, a), ws[3 * a + k], preferred_element_type=f32
                )
        result = (window(middle, 1).astype(f32) + jax.nn.silu(summed)).astype(bf16)
        result = result.reshape(many, count, groups, pixels, channels)
        for i, j in enumerate(which):
            for c in range(count):
                spatial[first + c, :, j] = result[i, c]

    def outward(c, peer, slot, source):
        count = ours - 1
        return remote(
            spatial.at[c, peer, pl.ds(1, count)], held.at[c, pl.ds(ours * source + 1, count)],
            send_sem.at[c, slot], recv_sem.at[c, source], 2 * peer + part,
        )

    def tailward(c, peer, slot, source):
        frame = lax.rem(ours * (source + 1), total)
        return remote(
            spatial.at[c, peer, ours], held.at[c, frame],
            tail_send.at[c, slot], tail_recv.at[c, source], 2 * peer + part,
        )

    def headward(c, peer, slot):
        return remote(
            spatial.at[c, peer, 0], held.at[c, 0], head_send.at[c, slot], head_recv.at[c], 2 * peer + part
        )

    def homeward(c, peer, slot, source, side, line):
        return remote(
            done.at[c, peer], y_ref.at[side, c, line], back_sem.at[c, slot], home_sem.at[c, source], peer
        )

    def stay(c):
        return pltpu.make_async_copy(done.at[c, me], y_ref.at[part, c, group], home_sem.at[c, me])

    def others(act):
        def step(k, _):
            act(k, lax.rem(group + k, groups), lax.rem(group + groups - k, groups))
            return 0

        lax.fori_loop(1, groups, step, 0)

    def scatter(c):
        others(lambda k, peer, source: outward(c, peer, k, group).start())

    def scatter_late(c):
        @pl.when(has_next)
        def _():
            others(lambda k, peer, source: tailward(c, peer, k, group).start())

        @pl.when(starts_clip)
        def _():
            others(lambda k, peer, source: headward(c, peer, k).start())

    def attend(c):
        held[c, pl.ds(ours * group + 1, ours - 1)] = spatial[c, group, 1:ours]

        @pl.when(has_next)
        def _():
            held[c, ours * group + ours] = spatial[c, group, ours]

        @pl.when(starts_clip)
        def _():
            held[c, 0] = spatial[c, group, 0]

        def arrive(k, peer, source):
            outward(c, peer, k, source).wait_recv()

            @pl.when(source < groups - 1)
            def _():
                tailward(c, peer, k, source).wait_recv()

        others(arrive)

        @pl.when(has_before)
        def _():
            headward(c, 0, 0).wait_recv()

        place = lax.broadcasted_iota(jnp.int32, (rows, rows), 0)
        other = lax.broadcasted_iota(jnp.int32, (rows, rows), 1)
        allowed = (lax.rem(place, pixels) == lax.rem(other, pixels)) & (other <= place)
        wide = held[c].reshape(rows, channels).astype(f32)
        scale = lax.rsqrt(jnp.mean(wide * wide, axis=-1, keepdims=True) + epsilon)
        normed = (wide * scale * gain[...]).astype(bf16)
        query = jnp.dot(normed, wq[...], preferred_element_type=f32).astype(bf16)
        key = jnp.dot(normed, wk[...], preferred_element_type=f32).astype(bf16)
        value = jnp.dot(normed, wv[...], preferred_element_type=f32).astype(bf16)
        scores = lax.dot_general(
            query, key, (((1,), (1,)), ((), ())), preferred_element_type=f32
        ) * channels ** (-0.5)
        scores = jnp.where(allowed, scores, -1e30)
        largest = jnp.max(scores, axis=-1, keepdims=True)
        probs = jnp.exp(scores - largest)
        probs = (probs / jnp.sum(probs, axis=-1, keepdims=True)).astype(bf16)
        context = jnp.dot(probs, value, preferred_element_type=f32).astype(bf16)
        mixed = jnp.dot(context, wo[...], preferred_element_type=f32)
        result = (wide + mixed).astype(bf16)
        done[c] = result.reshape(owners, halves, pixels, channels)

        def back(k, _):
            homeward(c, lax.rem(me + k, owners), k, me, part, group).start()
            return 0

        lax.fori_loop(1, owners, back, 0)
        stay(c).start()

    for b in range(chunks + lead):
        if b < chunks:
            trade(0, b).start()
        if b >= lead:
            trade(1, b - lead).start()
    loads[0].wait()
    for b in range(chunks):
        @pl.when(lower)
        def _():
            send_up(b)

        @pl.when(upper)
        def _():
            send_down(b)
    for load in loads[1:]:
        load.wait()

    for first, then, semaphore, peer in (
        (has_before, has_next, from_below, above), (has_next, has_before, from_above, below)
    ):
        @pl.when(first)
        def _():
            pl.semaphore_wait(semaphore, 1)

        @pl.when(then)
        def _():
            tell(semaphore, peer)

    tell(from_partner, partner)
    pl.semaphore_wait(from_partner, 1)

    final = 2 * frames
    main, ends = tuple(range(1, ours)), (0, ours)
    steps = chunks + chunks // joint

    def late(step, which, lifts, first):
        span = starts[first], starts[first + joint]
        lift(lifts, *span)
        reduce_rows(step, which, *span)
        shift_rows(step, which, *span)
        convolve_chunks(which, first, joint)

    for b in range(lead):
        pass_up(b)
    for b in range(chunks):
        pass_up(b + lead)
        trade(1, b).wait_recv()
        pass_down(b)

        @pl.when(has_before)
        def _():
            upward(b).wait_recv()

        lift(range(1, final), starts[b], starts[b + 1])
        reduce_rows(b, main, starts[b], starts[b + 1])
        shift_rows(b, main, starts[b], starts[b + 1])
        convolve_chunks(main, b, 1)
        scatter(b)
    for first in range(0, chunks, joint):
        step = chunks + first // joint

        @pl.when(has_next)
        def _():
            for d in range(first, first + joint):
                downward(d).wait_recv()

        @pl.when(starts_clip)
        def _():
            late(step, ends, (0, final, final + 1), first)

        @pl.when(has_before & has_next)
        def _():
            late(step, ends[1:], (final, final + 1), first)

        for c in range(first, first + joint):
            scatter_late(c)
        if first:
            for c in range(first - joint, first):
                attend(c)
    for c in range(chunks - joint, chunks):
        attend(c)

    for b in range(chunks):
        for i in range(2):
            trade(i, b).wait_send()

        @pl.when(has_next)
        def _():
            upward(b).wait_send()

        @pl.when(has_before)
        def _():
            downward(b).wait_send()

    for step in range(steps):
        kinds = ((len(main), col >= 0),)
        if step >= chunks:
            kinds = ((2, starts_clip), (1, has_before & has_next))
        for many, chosen in kinds:
            for side in range(2):
                @pl.when(sends_side[side] & chosen)
                def _():
                    sideways(step, many, side).wait_send()

    for c in range(chunks):
        others(lambda k, peer, source: outward(c, peer, k, group).wait_send())

        @pl.when(has_next)
        def _():
            others(lambda k, peer, source: tailward(c, peer, k, group).wait_send())

        @pl.when(starts_clip)
        def _():
            others(lambda k, peer, source: headward(c, peer, k).wait_send())

        def finish(k, _):
            peer, source = lax.rem(me + k, owners), lax.rem(me + owners - k, owners)
            homeward(c, peer, k, me, part, group).wait_send()
            homeward(c, peer, k, source, lax.rem(source, 2), lax.div(source, 2)).wait_recv()
            return 0

        lax.fori_loop(1, owners, finish, 0)
        stay(c).wait()


def per_device(
    video, w_time, b_time, w_down, b_down, w_space, b_space, gain, w_query, w_key, w_value, w_out
):
    frames, height, strip, channels = video.shape
    halves, owners = frames // 2, lax.axis_size("tm")
    groups, half = owners // 2, height // 2
    owned = half * strip // groups
    pixels = min(16, owned)
    chunks = owned // pixels
    deep, slots = half + 2, 2 * halves + 1
    joint = 2 if chunks % 2 == 0 else 1
    padded = -(-(joint * half // chunks + 2) // 8) * 8
    steps = chunks + chunks // joint
    vmem = pl.BlockSpec(memory_space=pltpu.VMEM)
    hbm = pl.BlockSpec(memory_space=pltpu.HBM)
    bf16 = jnp.bfloat16
    square = (channels, channels)
    shifted = pltpu.VMEM((slots, deep, strip, channels), bf16)
    flat = lambda v: v.reshape(1, channels)
    sems = pltpu.SemaphoreType.DMA
    result = pl.pallas_call(
        block_kernel,
        out_shape=jax.ShapeDtypeStruct((2, chunks, groups, halves, pixels, channels), bf16),
        in_specs=[hbm, hbm, vmem, hbm, vmem, hbm, vmem, vmem, hbm, hbm, hbm, hbm],
        out_specs=hbm,
        scratch_shapes=[
            pltpu.VMEM((3,) + square, bf16),
            pltpu.VMEM((3,) + square, bf16),
            pltpu.VMEM((9,) + square, bf16),
            pltpu.VMEM(square, bf16),
            pltpu.VMEM(square, bf16),
            pltpu.VMEM(square, bf16),
            pltpu.VMEM(square, bf16),
            pltpu.VMEM((2 * frames + 4, deep, strip, channels), bf16),
            pltpu.VMEM((2 * frames + 3, deep, strip, channels), bf16),
            shifted,
            shifted,
            shifted,
            pltpu.VMEM((steps, 2, slots, padded, channels), bf16),
            pltpu.VMEM((steps, 2, slots, padded, channels), bf16),
            pltpu.VMEM((chunks, groups, slots, pixels, channels), bf16),
            pltpu.VMEM((chunks, owners * halves, pixels, channels), bf16),
            pltpu.VMEM((chunks, owners, halves, pixels, channels), bf16),
            sems((8,)),
            sems((2, chunks)),
            sems((2, chunks)),
            sems((chunks,)),
            sems((chunks,)),
            sems((chunks,)),
            sems((chunks,)),
            sems((steps, 2)),
            sems((steps, 2)),
            sems((chunks, groups)),
            sems((chunks, groups)),
            sems((chunks, groups)),
            sems((chunks, groups)),
            sems((chunks, groups)),
            sems((chunks,)),
            sems((chunks, owners)),
            sems((chunks, owners)),
            pltpu.SemaphoreType.REGULAR,
            pltpu.SemaphoreType.REGULAR,
            pltpu.SemaphoreType.REGULAR,
        ],
        compiler_params=pltpu.CompilerParams(
            collective_id=0, has_side_effects=True, vmem_limit_bytes=57 * 1024 * 1024
        ),
    )(
        video, w_time, flat(b_time), w_down, flat(b_down),
        w_space, flat(b_space), flat(gain), w_query, w_key, w_value, w_out,
    )
    return result.transpose(3, 0, 1, 2, 4, 5).reshape(halves, height, strip, channels)


def solution(mesh):
    return jax.shard_map(
        per_device,
        mesh=mesh,
        in_specs=(P(("clips", "tm"), None, "cols", None),) + (P(),) * 11,
        out_specs=P(("clips", "tm"), None, "cols", None),
        check_vma=False,
    )
```

```python
import jax
import jax.numpy as jnp
from jax import lax
from jax.experimental import pallas as pl
from jax.experimental.pallas import tpu as pltpu
from jax.sharding import PartitionSpec as P

epsilon = 1e-06
MESH = pl.DeviceIdType.MESH


def block_kernel(
    video_hbm, wt_hbm, bt, wd_hbm, bd, ws_hbm, bs, gain, wq_hbm, wk_hbm, wv_hbm, wo_hbm, y_ref,
    wt, wd, ws, wq, wk, wv, wo, video, lifted, left_of, middle, right_of,
    edges, halo, spatial, held, done,
    load_sem, trade_send, trade_recv, up_send, up_recv, down_send, down_recv, edge_send, edge_recv,
    send_sem, recv_sem, tail_send, tail_recv, head_send, head_recv, back_sem, home_sem,
    from_below, from_above, from_partner,
):
    frames, height, strip, channels = video_hbm.shape
    _, chunks, groups, halves, pixels, _ = y_ref.shape
    owners, ours = 2 * groups, 2 * halves
    total = groups * ours
    rows = total * pixels
    half = height // 2
    lines = half // chunks
    padded = edges.shape[3]
    joint = 2 if chunks % 2 == 0 else 1
    me, col, cols = lax.axis_index("tm"), lax.axis_index("cols"), lax.axis_size("cols")
    group, part = lax.div(me, 2), lax.rem(me, 2)
    f32, bf16 = jnp.float32, jnp.bfloat16
    deep = half + 2
    starts = [0] + [lines * (b + 1) + 2 for b in range(chunks)]
    cuts = starts[:-1] + [half + 1]
    offset = 1 - part
    lead = min(1, chunks)

    loads = [
        pltpu.make_async_copy(source, target, load_sem.at[i])
        for i, (source, target) in enumerate(
            (
                (
                    video_hbm.at[:, pl.ds((half - 1) * part, half + 1)],
                    video.at[pl.ds(2 + frames * part, frames), pl.ds(offset, half + 1)],
                ),
                (wt_hbm, wt), (wd_hbm, wd), (ws_hbm, ws),
                (wq_hbm, wq), (wk_hbm, wk), (wv_hbm, wv), (wo_hbm, wo),
            )
        )
    ]
    for load in loads:
        load.start()

    barrier = pltpu.get_barrier_semaphore()

    upper, lower = part == 0, part == 1
    has_next, has_before = group < groups - 1, group > 0

    def tell(semaphore, peer):
        pl.semaphore_signal(semaphore, inc=1, device_id={"tm": peer}, device_id_type=MESH)

    partner = me + 1 - 2 * part
    above, below = lax.rem(me + 2, owners), lax.rem(me + owners - 2, owners)
    tell(barrier, partner)

    @pl.when(has_next)
    def _():
        tell(barrier, above)

    @pl.when(has_before)
    def _():
        tell(barrier, below)

    def greet_side(k, _):
        peer = lax.rem(col + k, cols)
        pl.semaphore_signal(barrier, inc=1, device_id={"cols": peer}, device_id_type=MESH)
        return 0

    lax.fori_loop(1, cols, greet_side, 0)

    starts_clip = group == 0
    slots = video.shape[0]
    for part_of, line in ((upper, 0), (lower, deep - 1)):
        @pl.when(part_of)
        def _():
            video[:, line] = jnp.zeros((slots, strip, channels), bf16)

    @pl.when(starts_clip)
    def _():
        video[0:2] = jnp.zeros((2, deep, strip, channels), bf16)
        lifted[0] = jnp.zeros((deep, strip, channels), bf16)

    @pl.when(jnp.logical_not(has_next))
    def _():
        video[slots - 2 :] = jnp.zeros((2, deep, strip, channels), bf16)

    pl.semaphore_wait(barrier, cols + jnp.where(has_next, 1, 0) + jnp.where(has_before, 1, 0))

    def remote(source, target, sent, landed, peer):
        return pltpu.make_async_remote_copy(
            src_ref=source, dst_ref=target, send_sem=sent, recv_sem=landed,
            device_id={"tm": peer}, device_id_type=MESH,
        )

    def trade(i, b):
        first, count = (frames - 1, 1) if i == 0 else (0, frames - 1)
        size = cuts[b + 1] - cuts[b]
        return remote(
            video_hbm.at[pl.ds(first, count), pl.ds((half - 1) * (1 - part) + cuts[b], size)],
            video.at[pl.ds(2 + frames * part + first, count), pl.ds(part + cuts[b], size)],
            trade_send.at[i, b], trade_recv.at[i, b], me + 1 - 2 * part,
        )

    def upward(b):
        size = pl.ds(offset + cuts[b], cuts[b + 1] - cuts[b])
        peer = lax.rem(me + 2, owners)
        return remote(video.at[2 * frames + 1, size], video.at[1, size], up_send.at[b], up_recv.at[b], peer)

    def downward(b):
        size = pl.ds(offset + cuts[b], cuts[b + 1] - cuts[b])
        peer = lax.rem(me + owners - 2, owners)
        return remote(
            video.at[pl.ds(2, 2), size], video.at[pl.ds(slots - 2, 2), size],
            down_send.at[b], down_recv.at[b], peer,
        )

    def send_up(b):
        @pl.when(has_next)
        def _():
            upward(b).start()

    def send_down(b):
        @pl.when(has_before)
        def _():
            downward(b).start()

    def pass_up(b):
        if b < chunks:
            trade(0, b).wait_recv()

            @pl.when(upper)
            def _():
                send_up(b)

    def pass_down(b):
        @pl.when(lower)
        def _():
            send_down(b)

    def stacked(ref, which, first, last):
        size = (last - first) * strip
        return jnp.concatenate([ref[f, first:last].reshape(size, channels) for f in which], 0)

    def lift(which, first, last):
        count = last - first
        size = count * strip
        own = [f + 2 for f in which]
        summed = jnp.dot(stacked(video, own, first, last), wt[0], preferred_element_type=f32)
        for k in (1, 2):
            summed = summed + jnp.dot(
                stacked(video, [f - k for f in own], first, last), wt[k], preferred_element_type=f32
            )
        summed = summed + bt[...]
        result = (stacked(video, own, first, last).astype(f32) + jax.nn.silu(summed)).astype(bf16)
        for i, f in enumerate(which):
            lifted[f + 1, first:last] = result[i * size : (i + 1) * size].reshape(count, strip, channels)

    def sideways(step, many, side):
        peer = lax.rem(col + 1, cols) if side == 0 else lax.rem(col + cols - 1, cols)
        which = pl.ds(0, many)
        return pltpu.make_async_remote_copy(
            src_ref=edges.at[step, side, which], dst_ref=halo.at[step, side, which],
            send_sem=edge_send.at[step, side], recv_sem=edge_recv.at[step, side],
            device_id={"cols": peer}, device_id_type=MESH,
        )

    sends_side = (col < cols - 1, col > 0)
    takes_side = (col > 0, col < cols - 1)

    def reduce_rows(step, which, first, last):
        count, many = last - first, len(which)
        size = count * strip
        summed = jnp.zeros((many * size, channels), f32) + bd[...]
        for k in range(3):
            summed = summed + jnp.dot(
                stacked(lifted, [2 * j + 2 - k for j in which], first, last), wd[k],
                preferred_element_type=f32,
            )
        reduced = summed.astype(bf16)
        for i, j in enumerate(which):
            middle[j, first:last] = reduced[i * size : (i + 1) * size].reshape(count, strip, channels)
            for chosen, line in ((upper, 0), (lower, deep - 1)):
                if first <= line < last:
                    @pl.when(chosen)
                    def _():
                        middle[j, line] = jnp.zeros((strip, channels), bf16)
        wide = stacked(middle, which, first, last).astype(f32).reshape(many, count, strip, channels)
        rest = jnp.zeros((many, padded - count, channels), f32)
        for side, place in ((0, strip - 1), (1, 0)):
            column = wide[:, :, place]
            column = jnp.concatenate([column, rest], 1) if padded > count else column
            edges[step, side, :many] = column.astype(bf16)
        for side in range(2):
            @pl.when(sends_side[side])
            def _():
                sideways(step, many, side).start()

    def shift_rows(step, which, first, last):
        count, many = last - first, len(which)
        part_size = count * strip
        size = many * part_size
        for side in range(2):
            @pl.when(takes_side[side])
            def _():
                sideways(step, many, side).wait_recv()

            @pl.when(jnp.logical_not(takes_side[side]))
            def _():
                halo[step, side, :many] = jnp.zeros((many, padded, channels), bf16)

        wide = stacked(middle, which, first, last).astype(f32)
        place = lax.rem(lax.broadcasted_iota(jnp.int32, (size, channels), 0), strip)

        def spread(side):
            column = halo[step, side, :many].astype(f32)[:, :count]
            column = jnp.broadcast_to(column[:, :, None, :], (many, count, strip, channels))
            return column.reshape(size, channels)

        before = jnp.where(place == 0, spread(0), pltpu.roll(wide, 1, 0)).astype(bf16)
        after = jnp.where(place == strip - 1, spread(1), pltpu.roll(wide, size - 1, 0)).astype(bf16)
        for i, j in enumerate(which):
            own = slice(i * part_size, (i + 1) * part_size)
            left_of[j, first:last] = before[own].reshape(count, strip, channels)
            right_of[j, first:last] = after[own].reshape(count, strip, channels)

    def convolve_chunks(which, first, count):
        top, deep_rows = first * lines, count * lines
        many = len(which)

        def window(ref, a):
            return stacked(ref, which, top + a, top + a + deep_rows)

        summed = jnp.zeros((many * deep_rows * strip, channels), f32) + bs[...]
        for k, shifted in ((1, middle), (0, left_of), (2, right_of)):
            for a in range(3):
                summed = summed + jnp.dot(
                    window(shifted, a), ws[3 * a + k], preferred_element_type=f32
                )
        result = (window(middle, 1).astype(f32) + jax.nn.silu(summed)).astype(bf16)
        result = result.reshape(many, count, groups, pixels, channels)
        for i, j in enumerate(which):
            for c in range(count):
                spatial[first + c, :, j] = result[i, c]

    def outward(c, peer, slot, source):
        count = ours - 1
        return remote(
            spatial.at[c, peer, pl.ds(1, count)], held.at[c, pl.ds(ours * source + 1, count)],
            send_sem.at[c, slot], recv_sem.at[c, source], 2 * peer + part,
        )

    def tailward(c, peer, slot, source):
        frame = lax.rem(ours * (source + 1), total)
        return remote(
            spatial.at[c, peer, ours], held.at[c, frame],
            tail_send.at[c, slot], tail_recv.at[c, source], 2 * peer + part,
        )

    def headward(c, peer, slot):
        return remote(
            spatial.at[c, peer, 0], held.at[c, 0], head_send.at[c, slot], head_recv.at[c], 2 * peer + part
        )

    def homeward(c, peer, slot, source, side, line):
        return remote(
            done.at[c, peer], y_ref.at[side, c, line], back_sem.at[c, slot], home_sem.at[c, source], peer
        )

    def stay(c):
        return pltpu.make_async_copy(done.at[c, me], y_ref.at[part, c, group], home_sem.at[c, me])

    def others(act):
        def step(k, _):
            act(k, lax.rem(group + k, groups), lax.rem(group + groups - k, groups))
            return 0

        lax.fori_loop(1, groups, step, 0)

    def scatter(c):
        others(lambda k, peer, source: outward(c, peer, k, group).start())

    def scatter_late(c):
        @pl.when(has_next)
        def _():
            others(lambda k, peer, source: tailward(c, peer, k, group).start())

        @pl.when(starts_clip)
        def _():
            others(lambda k, peer, source: headward(c, peer, k).start())

    def attend(c):
        held[c, pl.ds(ours * group + 1, ours - 1)] = spatial[c, group, 1:ours]

        @pl.when(has_next)
        def _():
            held[c, ours * group + ours] = spatial[c, group, ours]

        @pl.when(starts_clip)
        def _():
            held[c, 0] = spatial[c, group, 0]

        def arrive(k, peer, source):
            outward(c, peer, k, source).wait_recv()

            @pl.when(source < groups - 1)
            def _():
                tailward(c, peer, k, source).wait_recv()

        others(arrive)

        @pl.when(has_before)
        def _():
            headward(c, 0, 0).wait_recv()

        place = lax.broadcasted_iota(jnp.int32, (rows, rows), 0)
        other = lax.broadcasted_iota(jnp.int32, (rows, rows), 1)
        allowed = (lax.rem(place, pixels) == lax.rem(other, pixels)) & (other <= place)
        wide = held[c].reshape(rows, channels).astype(f32)
        scale = lax.rsqrt(jnp.mean(wide * wide, axis=-1, keepdims=True) + epsilon)
        normed = (wide * scale * gain[...]).astype(bf16)
        query = jnp.dot(normed, wq[...], preferred_element_type=f32).astype(bf16)
        key = jnp.dot(normed, wk[...], preferred_element_type=f32).astype(bf16)
        value = jnp.dot(normed, wv[...], preferred_element_type=f32).astype(bf16)
        scores = lax.dot_general(
            query, key, (((1,), (1,)), ((), ())), preferred_element_type=f32
        ) * channels ** (-0.5)
        scores = jnp.where(allowed, scores, -1e30)
        largest = jnp.max(scores, axis=-1, keepdims=True)
        probs = jnp.exp(scores - largest)
        probs = (probs / jnp.sum(probs, axis=-1, keepdims=True)).astype(bf16)
        context = jnp.dot(probs, value, preferred_element_type=f32).astype(bf16)
        mixed = jnp.dot(context, wo[...], preferred_element_type=f32)
        result = (wide + mixed).astype(bf16)
        done[c] = result.reshape(owners, halves, pixels, channels)

        def back(k, _):
            homeward(c, lax.rem(me + k, owners), k, me, part, group).start()
            return 0

        lax.fori_loop(1, owners, back, 0)
        stay(c).start()

    for b in range(chunks):
        for i in range(2):
            trade(i, b).start()
    loads[0].wait()
    for b in range(chunks):
        @pl.when(lower)
        def _():
            send_up(b)

        @pl.when(upper)
        def _():
            send_down(b)
    for load in loads[1:]:
        load.wait()

    for first, then, semaphore, peer in (
        (has_before, has_next, from_below, above), (has_next, has_before, from_above, below)
    ):
        @pl.when(first)
        def _():
            pl.semaphore_wait(semaphore, 1)

        @pl.when(then)
        def _():
            tell(semaphore, peer)

    tell(from_partner, partner)
    pl.semaphore_wait(from_partner, 1)

    final = 2 * frames
    main, ends = tuple(range(1, ours)), (0, ours)
    steps = chunks + chunks // joint

    def late(step, which, lifts, first):
        span = starts[first], starts[first + joint]
        lift(lifts, *span)
        reduce_rows(step, which, *span)
        shift_rows(step, which, *span)
        convolve_chunks(which, first, joint)

    pass_up(0)
    ready = [frames * part + f for f in range(2, frames)]
    waiting = [1, frames, frames + 1] + [frames * (1 - part) + f for f in range(2, frames)]
    lift(ready, 0, deep)
    for b in range(chunks):
        trade(1, b).wait_recv()
        pass_down(b)

        @pl.when(has_before)
        def _():
            upward(b).wait_recv()

        lift(waiting, starts[b], starts[b + 1])
        reduce_rows(b, main, starts[b], starts[b + 1])
        pass_up(b + 1)
        shift_rows(b, main, starts[b], starts[b + 1])
        convolve_chunks(main, b, 1)
        scatter(b)
    for first in range(0, chunks, joint):
        step = chunks + first // joint

        @pl.when(has_next)
        def _():
            for d in range(first, first + joint):
                downward(d).wait_recv()

        @pl.when(starts_clip)
        def _():
            late(step, ends, (0, final, final + 1), first)

        @pl.when(has_before & has_next)
        def _():
            late(step, ends[1:], (final, final + 1), first)

        for c in range(first, first + joint):
            scatter_late(c)
        if first:
            for c in range(first - joint, first):
                attend(c)
    for c in range(chunks - joint, chunks):
        attend(c)

    for b in range(chunks):
        for i in range(2):
            trade(i, b).wait_send()

        @pl.when(has_next)
        def _():
            upward(b).wait_send()

        @pl.when(has_before)
        def _():
            downward(b).wait_send()

    for step in range(steps):
        kinds = ((len(main), col >= 0),)
        if step >= chunks:
            kinds = ((2, starts_clip), (1, has_before & has_next))
        for many, chosen in kinds:
            for side in range(2):
                @pl.when(sends_side[side] & chosen)
                def _():
                    sideways(step, many, side).wait_send()

    for c in range(chunks):
        others(lambda k, peer, source: outward(c, peer, k, group).wait_send())

        @pl.when(has_next)
        def _():
            others(lambda k, peer, source: tailward(c, peer, k, group).wait_send())

        @pl.when(starts_clip)
        def _():
            others(lambda k, peer, source: headward(c, peer, k).wait_send())

        def finish(k, _):
            peer, source = lax.rem(me + k, owners), lax.rem(me + owners - k, owners)
            homeward(c, peer, k, me, part, group).wait_send()
            homeward(c, peer, k, source, lax.rem(source, 2), lax.div(source, 2)).wait_recv()
            return 0

        lax.fori_loop(1, owners, finish, 0)
        stay(c).wait()


def per_device(
    video, w_time, b_time, w_down, b_down, w_space, b_space, gain, w_query, w_key, w_value, w_out
):
    frames, height, strip, channels = video.shape
    halves, owners = frames // 2, lax.axis_size("tm")
    groups, half = owners // 2, height // 2
    owned = half * strip // groups
    pixels = min(16, owned)
    chunks = owned // pixels
    deep, slots = half + 2, 2 * halves + 1
    joint = 2 if chunks % 2 == 0 else 1
    padded = -(-(joint * half // chunks + 2) // 8) * 8
    steps = chunks + chunks // joint
    vmem = pl.BlockSpec(memory_space=pltpu.VMEM)
    hbm = pl.BlockSpec(memory_space=pltpu.HBM)
    bf16 = jnp.bfloat16
    square = (channels, channels)
    shifted = pltpu.VMEM((slots, deep, strip, channels), bf16)
    flat = lambda v: v.reshape(1, channels)
    sems = pltpu.SemaphoreType.DMA
    result = pl.pallas_call(
        block_kernel,
        out_shape=jax.ShapeDtypeStruct((2, chunks, groups, halves, pixels, channels), bf16),
        in_specs=[hbm, hbm, vmem, hbm, vmem, hbm, vmem, vmem, hbm, hbm, hbm, hbm],
        out_specs=hbm,
        scratch_shapes=[
            pltpu.VMEM((3,) + square, bf16),
            pltpu.VMEM((3,) + square, bf16),
            pltpu.VMEM((9,) + square, bf16),
            pltpu.VMEM(square, bf16),
            pltpu.VMEM(square, bf16),
            pltpu.VMEM(square, bf16),
            pltpu.VMEM(square, bf16),
            pltpu.VMEM((2 * frames + 4, deep, strip, channels), bf16),
            pltpu.VMEM((2 * frames + 3, deep, strip, channels), bf16),
            shifted,
            shifted,
            shifted,
            pltpu.VMEM((steps, 2, slots, padded, channels), bf16),
            pltpu.VMEM((steps, 2, slots, padded, channels), bf16),
            pltpu.VMEM((chunks, groups, slots, pixels, channels), bf16),
            pltpu.VMEM((chunks, owners * halves, pixels, channels), bf16),
            pltpu.VMEM((chunks, owners, halves, pixels, channels), bf16),
            sems((8,)),
            sems((2, chunks)),
            sems((2, chunks)),
            sems((chunks,)),
            sems((chunks,)),
            sems((chunks,)),
            sems((chunks,)),
            sems((steps, 2)),
            sems((steps, 2)),
            sems((chunks, groups)),
            sems((chunks, groups)),
            sems((chunks, groups)),
            sems((chunks, groups)),
            sems((chunks, groups)),
            sems((chunks,)),
            sems((chunks, owners)),
            sems((chunks, owners)),
            pltpu.SemaphoreType.REGULAR,
            pltpu.SemaphoreType.REGULAR,
            pltpu.SemaphoreType.REGULAR,
        ],
        compiler_params=pltpu.CompilerParams(
            collective_id=0, has_side_effects=True, vmem_limit_bytes=57 * 1024 * 1024
        ),
    )(
        video, w_time, flat(b_time), w_down, flat(b_down),
        w_space, flat(b_space), flat(gain), w_query, w_key, w_value, w_out,
    )
    return result.transpose(3, 0, 1, 2, 4, 5).reshape(halves, height, strip, channels)


def solution(mesh):
    return jax.shard_map(
        per_device,
        mesh=mesh,
        in_specs=(P(("clips", "tm"), None, "cols", None),) + (P(),) * 11,
        out_specs=P(("clips", "tm"), None, "cols", None),
        check_vma=False,
    )
```

```python
import jax
import jax.numpy as jnp
from jax import lax
from jax.experimental import pallas as pl
from jax.experimental.pallas import tpu as pltpu
from jax.sharding import PartitionSpec as P

epsilon = 1e-06
MESH = pl.DeviceIdType.MESH


def block_kernel(
    video_hbm, wt_hbm, bt, wd_hbm, bd, ws_hbm, bs, gain, wq_hbm, wk_hbm, wv_hbm, wo_hbm, y_ref,
    wt, wd, ws, wq, wk, wv, wo, video, lifted, left_of, middle, right_of,
    edges, halo, spatial, held, done,
    load_sem, trade_send, trade_recv, up_send, up_recv, down_send, down_recv, edge_send, edge_recv,
    send_sem, recv_sem, tail_send, tail_recv, head_send, head_recv, back_sem, home_sem,
    from_below, from_above, from_partner,
):
    frames, height, strip, channels = video_hbm.shape
    _, chunks, groups, halves, pixels, _ = y_ref.shape
    owners, ours = 2 * groups, 2 * halves
    total = groups * ours
    rows = total * pixels
    half = height // 2
    lines = half // chunks
    padded = edges.shape[3]
    joint = 2 if chunks % 2 == 0 else 1
    me, col, cols = lax.axis_index("tm"), lax.axis_index("cols"), lax.axis_size("cols")
    group, part = lax.div(me, 2), lax.rem(me, 2)
    f32, bf16 = jnp.float32, jnp.bfloat16
    deep = half + 2
    starts = [0] + [lines * (b + 1) + 2 for b in range(chunks)]
    cuts = starts[:-1] + [half + 1]
    offset = 1 - part
    lead = min(1, chunks)

    loads = [
        pltpu.make_async_copy(source, target, load_sem.at[i])
        for i, (source, target) in enumerate(
            (
                (
                    video_hbm.at[:, pl.ds((half - 1) * part, half + 1)],
                    video.at[pl.ds(2 + frames * part, frames), pl.ds(offset, half + 1)],
                ),
                (wt_hbm, wt), (wd_hbm, wd), (ws_hbm, ws),
                (wq_hbm, wq), (wk_hbm, wk), (wv_hbm, wv), (wo_hbm, wo),
            )
        )
    ]
    for load in loads:
        load.start()

    barrier = pltpu.get_barrier_semaphore()

    upper, lower = part == 0, part == 1
    has_next, has_before = group < groups - 1, group > 0

    def tell(semaphore, peer):
        pl.semaphore_signal(semaphore, inc=1, device_id={"tm": peer}, device_id_type=MESH)

    partner = me + 1 - 2 * part
    above, below = lax.rem(me + 2, owners), lax.rem(me + owners - 2, owners)
    tell(barrier, partner)

    @pl.when(has_next)
    def _():
        tell(barrier, above)

    @pl.when(has_before)
    def _():
        tell(barrier, below)

    def greet_side(k, _):
        peer = lax.rem(col + k, cols)
        pl.semaphore_signal(barrier, inc=1, device_id={"cols": peer}, device_id_type=MESH)
        return 0

    lax.fori_loop(1, cols, greet_side, 0)

    starts_clip = group == 0
    slots = video.shape[0]
    for part_of, line in ((upper, 0), (lower, deep - 1)):
        @pl.when(part_of)
        def _():
            video[:, line] = jnp.zeros((slots, strip, channels), bf16)

    @pl.when(starts_clip)
    def _():
        video[0:2] = jnp.zeros((2, deep, strip, channels), bf16)
        lifted[0] = jnp.zeros((deep, strip, channels), bf16)

    @pl.when(jnp.logical_not(has_next))
    def _():
        video[slots - 2 :] = jnp.zeros((2, deep, strip, channels), bf16)

    pl.semaphore_wait(barrier, cols + jnp.where(has_next, 1, 0) + jnp.where(has_before, 1, 0))

    def remote(source, target, sent, landed, peer):
        return pltpu.make_async_remote_copy(
            src_ref=source, dst_ref=target, send_sem=sent, recv_sem=landed,
            device_id={"tm": peer}, device_id_type=MESH,
        )

    def trade(i, b):
        first, count = (frames - 1, 1) if i == 0 else (0, frames - 1)
        size = cuts[b + 1] - cuts[b]
        return remote(
            video_hbm.at[pl.ds(first, count), pl.ds((half - 1) * (1 - part) + cuts[b], size)],
            video.at[pl.ds(2 + frames * part + first, count), pl.ds(part + cuts[b], size)],
            trade_send.at[i, b], trade_recv.at[i, b], me + 1 - 2 * part,
        )

    def upward(b):
        size = pl.ds(offset + cuts[b], cuts[b + 1] - cuts[b])
        peer = lax.rem(me + 2, owners)
        return remote(video.at[2 * frames + 1, size], video.at[1, size], up_send.at[b], up_recv.at[b], peer)

    def downward(b):
        size = pl.ds(offset + cuts[b], cuts[b + 1] - cuts[b])
        peer = lax.rem(me + owners - 2, owners)
        return remote(
            video.at[pl.ds(2, 2), size], video.at[pl.ds(slots - 2, 2), size],
            down_send.at[b], down_recv.at[b], peer,
        )

    def send_up(b):
        @pl.when(has_next)
        def _():
            upward(b).start()

    def send_down(b):
        @pl.when(has_before)
        def _():
            downward(b).start()

    def pass_up(b):
        if b < chunks:
            trade(0, b).wait_recv()

            @pl.when(upper)
            def _():
                send_up(b)

    def pass_down(b):
        @pl.when(lower)
        def _():
            send_down(b)

    def stacked(ref, which, first, last):
        size = (last - first) * strip
        return jnp.concatenate([ref[f, first:last].reshape(size, channels) for f in which], 0)

    def lift(which, first, last):
        count = last - first
        size = count * strip
        own = [f + 2 for f in which]
        summed = jnp.dot(stacked(video, own, first, last), wt[0], preferred_element_type=f32)
        for k in (1, 2):
            summed = summed + jnp.dot(
                stacked(video, [f - k for f in own], first, last), wt[k], preferred_element_type=f32
            )
        summed = summed + bt[...]
        result = (stacked(video, own, first, last).astype(f32) + jax.nn.silu(summed)).astype(bf16)
        for i, f in enumerate(which):
            lifted[f + 1, first:last] = result[i * size : (i + 1) * size].reshape(count, strip, channels)

    def sideways(step, many, side):
        peer = lax.rem(col + 1, cols) if side == 0 else lax.rem(col + cols - 1, cols)
        which = pl.ds(0, many)
        return pltpu.make_async_remote_copy(
            src_ref=edges.at[step, side, which], dst_ref=halo.at[step, side, which],
            send_sem=edge_send.at[step, side], recv_sem=edge_recv.at[step, side],
            device_id={"cols": peer}, device_id_type=MESH,
        )

    sends_side = (col < cols - 1, col > 0)
    takes_side = (col > 0, col < cols - 1)

    def reduce_rows(step, which, first, last):
        count, many = last - first, len(which)
        size = count * strip
        summed = jnp.zeros((many * size, channels), f32) + bd[...]
        for k in range(3):
            summed = summed + jnp.dot(
                stacked(lifted, [2 * j + 2 - k for j in which], first, last), wd[k],
                preferred_element_type=f32,
            )
        reduced = summed.astype(bf16)
        for i, j in enumerate(which):
            middle[j, first:last] = reduced[i * size : (i + 1) * size].reshape(count, strip, channels)
            for chosen, line in ((upper, 0), (lower, deep - 1)):
                if first <= line < last:
                    @pl.when(chosen)
                    def _():
                        middle[j, line] = jnp.zeros((strip, channels), bf16)
        wide = stacked(middle, which, first, last).astype(f32).reshape(many, count, strip, channels)
        rest = jnp.zeros((many, padded - count, channels), f32)
        for side, place in ((0, strip - 1), (1, 0)):
            column = wide[:, :, place]
            column = jnp.concatenate([column, rest], 1) if padded > count else column
            edges[step, side, :many] = column.astype(bf16)
        for side in range(2):
            @pl.when(sends_side[side])
            def _():
                sideways(step, many, side).start()

    def shift_rows(step, which, first, last):
        count, many = last - first, len(which)
        part_size = count * strip
        size = many * part_size
        for side in range(2):
            @pl.when(takes_side[side])
            def _():
                sideways(step, many, side).wait_recv()

            @pl.when(jnp.logical_not(takes_side[side]))
            def _():
                halo[step, side, :many] = jnp.zeros((many, padded, channels), bf16)

        wide = stacked(middle, which, first, last).astype(f32)
        place = lax.rem(lax.broadcasted_iota(jnp.int32, (size, channels), 0), strip)

        def spread(side):
            column = halo[step, side, :many].astype(f32)[:, :count]
            column = jnp.broadcast_to(column[:, :, None, :], (many, count, strip, channels))
            return column.reshape(size, channels)

        before = jnp.where(place == 0, spread(0), pltpu.roll(wide, 1, 0)).astype(bf16)
        after = jnp.where(place == strip - 1, spread(1), pltpu.roll(wide, size - 1, 0)).astype(bf16)
        for i, j in enumerate(which):
            own = slice(i * part_size, (i + 1) * part_size)
            left_of[j, first:last] = before[own].reshape(count, strip, channels)
            right_of[j, first:last] = after[own].reshape(count, strip, channels)

    def convolve_chunks(which, first, count):
        top, deep_rows = first * lines, count * lines
        many = len(which)

        def window(ref, a):
            return stacked(ref, which, top + a, top + a + deep_rows)

        summed = jnp.zeros((many * deep_rows * strip, channels), f32) + bs[...]
        for k, shifted in ((1, middle), (0, left_of), (2, right_of)):
            for a in range(3):
                summed = summed + jnp.dot(
                    window(shifted, a), ws[3 * a + k], preferred_element_type=f32
                )
        result = (window(middle, 1).astype(f32) + jax.nn.silu(summed)).astype(bf16)
        result = result.reshape(many, count, groups, pixels, channels)
        for i, j in enumerate(which):
            for c in range(count):
                spatial[first + c, :, j] = result[i, c]

    def outward(c, peer, slot, source):
        count = ours - 1
        return remote(
            spatial.at[c, peer, pl.ds(1, count)], held.at[c, pl.ds(ours * source + 1, count)],
            send_sem.at[c, slot], recv_sem.at[c, source], 2 * peer + part,
        )

    def tailward(c, peer, slot, source):
        frame = lax.rem(ours * (source + 1), total)
        return remote(
            spatial.at[c, peer, ours], held.at[c, frame],
            tail_send.at[c, slot], tail_recv.at[c, source], 2 * peer + part,
        )

    def headward(c, peer, slot):
        return remote(
            spatial.at[c, peer, 0], held.at[c, 0], head_send.at[c, slot], head_recv.at[c], 2 * peer + part
        )

    def homeward(c, peer, slot, source, side, line):
        return remote(
            done.at[c, peer], y_ref.at[side, c, line], back_sem.at[c, slot], home_sem.at[c, source], peer
        )

    def stay(c):
        return pltpu.make_async_copy(done.at[c, me], y_ref.at[part, c, group], home_sem.at[c, me])

    def others(act):
        def step(k, _):
            act(k, lax.rem(group + groups - k, groups), lax.rem(group + k, groups))
            return 0

        lax.fori_loop(1, groups, step, 0)

    def scatter(c):
        others(lambda k, peer, source: outward(c, peer, k, group).start())

    def scatter_late(c):
        @pl.when(has_next)
        def _():
            others(lambda k, peer, source: tailward(c, peer, k, group).start())

        @pl.when(starts_clip)
        def _():
            others(lambda k, peer, source: headward(c, peer, k).start())

    def attend(c):
        held[c, pl.ds(ours * group + 1, ours - 1)] = spatial[c, group, 1:ours]

        @pl.when(has_next)
        def _():
            held[c, ours * group + ours] = spatial[c, group, ours]

        @pl.when(starts_clip)
        def _():
            held[c, 0] = spatial[c, group, 0]

        def arrive(k, peer, source):
            outward(c, peer, k, source).wait_recv()

            @pl.when(source < groups - 1)
            def _():
                tailward(c, peer, k, source).wait_recv()

        others(arrive)

        @pl.when(has_before)
        def _():
            headward(c, 0, 0).wait_recv()

        place = lax.broadcasted_iota(jnp.int32, (rows, rows), 0)
        other = lax.broadcasted_iota(jnp.int32, (rows, rows), 1)
        allowed = (lax.rem(place, pixels) == lax.rem(other, pixels)) & (other <= place)
        wide = held[c].reshape(rows, channels).astype(f32)
        scale = lax.rsqrt(jnp.mean(wide * wide, axis=-1, keepdims=True) + epsilon)
        normed = (wide * scale * gain[...]).astype(bf16)
        query = jnp.dot(normed, wq[...], preferred_element_type=f32).astype(bf16)
        key = jnp.dot(normed, wk[...], preferred_element_type=f32).astype(bf16)
        value = jnp.dot(normed, wv[...], preferred_element_type=f32).astype(bf16)
        scores = lax.dot_general(
            query, key, (((1,), (1,)), ((), ())), preferred_element_type=f32
        ) * channels ** (-0.5)
        scores = jnp.where(allowed, scores, -1e30)
        largest = jnp.max(scores, axis=-1, keepdims=True)
        probs = jnp.exp(scores - largest)
        probs = (probs / jnp.sum(probs, axis=-1, keepdims=True)).astype(bf16)
        context = jnp.dot(probs, value, preferred_element_type=f32).astype(bf16)
        mixed = jnp.dot(context, wo[...], preferred_element_type=f32)
        result = (wide + mixed).astype(bf16)
        done[c] = result.reshape(owners, halves, pixels, channels)

        def back(k, _):
            homeward(c, lax.rem(me + k, owners), k, me, part, group).start()
            return 0

        lax.fori_loop(1, owners, back, 0)
        stay(c).start()

    for b in range(chunks):
        for i in range(2):
            trade(i, b).start()
    loads[0].wait()
    for b in range(chunks):
        @pl.when(lower)
        def _():
            send_up(b)

        @pl.when(upper)
        def _():
            send_down(b)
    for load in loads[1:]:
        load.wait()

    for first, then, semaphore, peer in (
        (has_before, has_next, from_below, above), (has_next, has_before, from_above, below)
    ):
        @pl.when(first)
        def _():
            pl.semaphore_wait(semaphore, 1)

        @pl.when(then)
        def _():
            tell(semaphore, peer)

    tell(from_partner, partner)
    pl.semaphore_wait(from_partner, 1)

    final = 2 * frames
    main, ends = tuple(range(1, ours)), (0, ours)
    steps = chunks + chunks // joint

    def late(step, which, lifts, first):
        span = starts[first], starts[first + joint]
        lift(lifts, *span)
        reduce_rows(step, which, *span)
        shift_rows(step, which, *span)
        convolve_chunks(which, first, joint)

    pass_up(0)
    ready = [frames * part + f for f in range(2, frames)]
    waiting = [1, frames, frames + 1] + [frames * (1 - part) + f for f in range(2, frames)]
    lift(ready, 0, deep)
    for b in range(chunks):
        trade(1, b).wait_recv()
        pass_down(b)

        @pl.when(has_before)
        def _():
            upward(b).wait_recv()

        lift(waiting, starts[b], starts[b + 1])
        reduce_rows(b, main, starts[b], starts[b + 1])
        pass_up(b + 1)
        shift_rows(b, main, starts[b], starts[b + 1])
        convolve_chunks(main, b, 1)
        scatter(b)
    for first in range(0, chunks, joint):
        step = chunks + first // joint

        @pl.when(has_next)
        def _():
            for d in range(first, first + joint):
                downward(d).wait_recv()

        @pl.when(starts_clip)
        def _():
            late(step, ends, (0, final, final + 1), first)

        @pl.when(has_before & has_next)
        def _():
            late(step, ends[1:], (final, final + 1), first)

        for c in range(first, first + joint):
            scatter_late(c)
        if first:
            for c in range(first - joint, first):
                attend(c)
    for c in range(chunks - joint, chunks):
        attend(c)

    for b in range(chunks):
        for i in range(2):
            trade(i, b).wait_send()

        @pl.when(has_next)
        def _():
            upward(b).wait_send()

        @pl.when(has_before)
        def _():
            downward(b).wait_send()

    for step in range(steps):
        kinds = ((len(main), col >= 0),)
        if step >= chunks:
            kinds = ((2, starts_clip), (1, has_before & has_next))
        for many, chosen in kinds:
            for side in range(2):
                @pl.when(sends_side[side] & chosen)
                def _():
                    sideways(step, many, side).wait_send()

    for c in range(chunks):
        others(lambda k, peer, source: outward(c, peer, k, group).wait_send())

        @pl.when(has_next)
        def _():
            others(lambda k, peer, source: tailward(c, peer, k, group).wait_send())

        @pl.when(starts_clip)
        def _():
            others(lambda k, peer, source: headward(c, peer, k).wait_send())

        def finish(k, _):
            peer, source = lax.rem(me + k, owners), lax.rem(me + owners - k, owners)
            homeward(c, peer, k, me, part, group).wait_send()
            homeward(c, peer, k, source, lax.rem(source, 2), lax.div(source, 2)).wait_recv()
            return 0

        lax.fori_loop(1, owners, finish, 0)
        stay(c).wait()


def per_device(
    video, w_time, b_time, w_down, b_down, w_space, b_space, gain, w_query, w_key, w_value, w_out
):
    frames, height, strip, channels = video.shape
    halves, owners = frames // 2, lax.axis_size("tm")
    groups, half = owners // 2, height // 2
    owned = half * strip // groups
    pixels = min(16, owned)
    chunks = owned // pixels
    deep, slots = half + 2, 2 * halves + 1
    joint = 2 if chunks % 2 == 0 else 1
    padded = -(-(joint * half // chunks + 2) // 8) * 8
    steps = chunks + chunks // joint
    vmem = pl.BlockSpec(memory_space=pltpu.VMEM)
    hbm = pl.BlockSpec(memory_space=pltpu.HBM)
    bf16 = jnp.bfloat16
    square = (channels, channels)
    shifted = pltpu.VMEM((slots, deep, strip, channels), bf16)
    flat = lambda v: v.reshape(1, channels)
    sems = pltpu.SemaphoreType.DMA
    result = pl.pallas_call(
        block_kernel,
        out_shape=jax.ShapeDtypeStruct((2, chunks, groups, halves, pixels, channels), bf16),
        in_specs=[hbm, hbm, vmem, hbm, vmem, hbm, vmem, vmem, hbm, hbm, hbm, hbm],
        out_specs=hbm,
        scratch_shapes=[
            pltpu.VMEM((3,) + square, bf16),
            pltpu.VMEM((3,) + square, bf16),
            pltpu.VMEM((9,) + square, bf16),
            pltpu.VMEM(square, bf16),
            pltpu.VMEM(square, bf16),
            pltpu.VMEM(square, bf16),
            pltpu.VMEM(square, bf16),
            pltpu.VMEM((2 * frames + 4, deep, strip, channels), bf16),
            pltpu.VMEM((2 * frames + 3, deep, strip, channels), bf16),
            shifted,
            shifted,
            shifted,
            pltpu.VMEM((steps, 2, slots, padded, channels), bf16),
            pltpu.VMEM((steps, 2, slots, padded, channels), bf16),
            pltpu.VMEM((chunks, groups, slots, pixels, channels), bf16),
            pltpu.VMEM((chunks, owners * halves, pixels, channels), bf16),
            pltpu.VMEM((chunks, owners, halves, pixels, channels), bf16),
            sems((8,)),
            sems((2, chunks)),
            sems((2, chunks)),
            sems((chunks,)),
            sems((chunks,)),
            sems((chunks,)),
            sems((chunks,)),
            sems((steps, 2)),
            sems((steps, 2)),
            sems((chunks, groups)),
            sems((chunks, groups)),
            sems((chunks, groups)),
            sems((chunks, groups)),
            sems((chunks, groups)),
            sems((chunks,)),
            sems((chunks, owners)),
            sems((chunks, owners)),
            pltpu.SemaphoreType.REGULAR,
            pltpu.SemaphoreType.REGULAR,
            pltpu.SemaphoreType.REGULAR,
        ],
        compiler_params=pltpu.CompilerParams(
            collective_id=0, has_side_effects=True, vmem_limit_bytes=57 * 1024 * 1024
        ),
    )(
        video, w_time, flat(b_time), w_down, flat(b_down),
        w_space, flat(b_space), flat(gain), w_query, w_key, w_value, w_out,
    )
    return result.transpose(3, 0, 1, 2, 4, 5).reshape(halves, height, strip, channels)


def solution(mesh):
    return jax.shard_map(
        per_device,
        mesh=mesh,
        in_specs=(P(("clips", "tm"), None, "cols", None),) + (P(),) * 11,
        out_specs=P(("clips", "tm"), None, "cols", None),
        check_vma=False,
    )
```
